32 devices in a mesh: dp: 4 (over z), ctx: 8 (over y, x, core).
Axes of the slice: x: 2, y: 2, z: 4, core: 2. Of those that a mesh axis runs over, the one named last changes fastest.
Arguments:
- head_inputs: bfloat16 [4, 1024, 2048], P('dp', 'ctx'), may hold values from -11 to 11
- entry_operator: bfloat16 [4, 1024, 128], P('dp', 'ctx'), may hold values from -3 to 3
- memory_readout: bfloat16 [4, 1024, 128], P('dp', 'ctx'), may hold values from -0.1796875 to 0.1796875
- unshifted_strides: float32 [4, 64, 1024], P('dp', None, 'ctx'), may hold values from -1.5 to 5.5, as said below
- log_decay_rates: float32 [64], P('dp'), may hold values from -11 to -2
- stride_shift: float32 [64], P('dp'), may hold values from -0.5 to 0.5
- bypass_coefficients: float32 [64], P('dp'), may hold values from 0.5 to 1.5
- result_cotangent: bfloat16 [4, 1024, 2048], P('dp', 'ctx'), may hold values from -26 to 26
Outputs:
- output: bfloat16 [4, 1024, 2048], P('dp', 'ctx')
- channels_grad: bfloat16 [4, 1024, 2048], P('dp', 'ctx')
- input_map_grad: float32 [4, 1024, 128], P('dp', 'ctx')
- output_map_grad: float32 [4, 1024, 128], P('dp', 'ctx')
- timestep_raw_gradient: float32 [4, 64, 1024], P('dp', None, 'ctx')
- a_log_grad: float32 [64], P('dp')
- bias_grad: float32 [64], P('dp')
- skip_grad: float32 [64], P('dp')
The draws below stay inside these ranges and needn't reach their ends.
Inputs may be any that keep to these rules, and one draw needn't show every extreme that they name: `unshifted_strides`: step sizes are moderate at most positions, with a few large ones in each sequence.
All inputs are finite; a program needn't handle non-finite values.
Results may differ from the reference program's by a relative error of at most 0.001.
Values sent between devices are 32-bit elements; how exact they have to be, the bound alone decides.
No kernel may reach another device: no remote copies, remote signals or barrier semaphores. Data moves between devices by JAX's collectives and lax.ppermute only.
A program may use at most 128 MiB of HBM per device.

```python
import jax
import jax.numpy as jnp
from jax import lax

HEADS = 64
HEAD_DIM = 32
MEMORY_WIDTH = 128
TOK_DEV = 128
WINDOW_LENGTH = 1024
BATCH_COUNT = 4


def block_levels(key):
    level_key = jax.random.fold_in(key, 71)
    blocks = WINDOW_LENGTH // TOK_DEV
    exponent = jax.random.uniform(level_key, (BATCH_COUNT, blocks), jnp.float32, -2.5, 1.0)
    return jnp.repeat(jnp.exp(exponent), TOK_DEV, axis=1)


def draw_head_inputs(key, part):
    first = jax.random.fold_in(key, 53)
    shape = (BATCH_COUNT, WINDOW_LENGTH, HEADS * HEAD_DIM)
    noise = jnp.clip(jax.random.normal(first, shape, jnp.float32), -4.0, 4.0)
    levels = block_levels(key)
    return (noise * levels[:, :, None]).astype(jnp.bfloat16)


def draw_entry_operator(key, part):
    first = jax.random.fold_in(key, 59)
    shape = (BATCH_COUNT, WINDOW_LENGTH, MEMORY_WIDTH)
    noise = jnp.clip(jax.random.normal(first, shape, jnp.float32), -4.0, 4.0)
    levels = block_levels(key)
    value = noise * MEMORY_WIDTH ** (-0.5) * levels[:, :, None]
    return value.astype(jnp.bfloat16)


def draw_log_decay_rates(key, part):
    first, second = jax.random.split(jax.random.fold_in(key, 11), 2)
    spread = jax.random.uniform(first, (HEADS,), jnp.float32)
    ranks = jax.random.permutation(second, HEADS)
    quick_count = HEADS // 4
    middle_count = HEADS // 4
    quick = ranks < quick_count
    middle = jnp.logical_and(ranks >= quick_count, ranks < quick_count + middle_count)
    slow_rate = jnp.log(0.2 / WINDOW_LENGTH) + spread * jnp.log(10.0)
    quick_rate = jnp.log(0.035) + spread * jnp.log(2.0)
    middle_rate = jnp.log(0.0105) + spread * jnp.log(1.45)
    value = jnp.where(quick, quick_rate, jnp.where(middle, middle_rate, slow_rate))
    return value.astype(jnp.float32)


def draw_unshifted_strides(key, part):
    first, second = jax.random.split(jax.random.fold_in(key, 23), 2)
    starting_index = jnp.clip(0.5 * jax.random.normal(first, (BATCH_COUNT, HEADS, WINDOW_LENGTH), jnp.float32), -1.0, 1.0) - 0.5
    worker_places = jax.random.randint(second, (BATCH_COUNT, 4), 0, WINDOW_LENGTH)
    index_table = jnp.arange(WINDOW_LENGTH, dtype=jnp.int32)
    contiguous_spans = jnp.any(index_table[None, None, :] == worker_places[:, :, None], axis=1).astype(jnp.float32)
    return (starting_index + 4.0 * contiguous_spans[:, None, :]).astype(jnp.float32)


def draw_result_cotangent(key, part):
    first = jax.random.fold_in(key, 37)
    noise = jnp.clip(jax.random.normal(first, (BATCH_COUNT, WINDOW_LENGTH, HEADS * HEAD_DIM), jnp.float32), -4.0, 4.0)
    along = jnp.arange(WINDOW_LENGTH, dtype=jnp.float32) / (WINDOW_LENGTH - 1)
    spanning_parts = jnp.arange(BATCH_COUNT, dtype=jnp.float32) / max(BATCH_COUNT - 1, 1)
    ramp = 1.0 + 2.0 * along
    value = noise * ramp[None, :, None] * (1.0 + spanning_parts)[:, None, None]
    return value.astype(jnp.bfloat16)


def steps_of(key, shape, pieces, smallest, top_value):
    loudness = 1.0
    for position, parts in pieces:
        draws = jax.random.uniform(jax.random.fold_in(jax.random.fold_in(key, 6), position), (parts,), jnp.float32, smallest / len(pieces), top_value / len(pieces))
        loudness = loudness * jnp.repeat(jnp.exp(draws), shape[position] // parts).reshape((-1,) + (1,) * (len(shape) - 1 - position))
    return loudness


def scatter_about(rng, dims, scale, bound, pieces=(), kind=jnp.bfloat16):
    values = jax.random.normal(rng, dims, jnp.float32) * scale
    if len(pieces) > 0:
        values = steps_of(rng, dims, pieces, -0.22, 0.18) * values
    return jnp.clip(values, min=-bound, max=bound).astype(kind)


def setup_inputs(seed: int = 0) -> dict:
    key_list = jax.random.split(jax.random.key(seed), 9)
    head_inputs = draw_head_inputs(jax.random.fold_in(key_list[8], 71), 0)
    entry_operator = draw_entry_operator(jax.random.fold_in(key_list[8], 71), 0)
    memory_readout = scatter_about(key_list[2], (BATCH_COUNT, WINDOW_LENGTH, MEMORY_WIDTH), 0.03, 0.1796875, ((0, 4), (1, 8)))
    unshifted_strides = draw_unshifted_strides(jax.random.fold_in(key_list[8], 71), 0)
    log_decay_rates = draw_log_decay_rates(jax.random.fold_in(key_list[8], 71), 0)
    stride_shift = jnp.clip(jax.random.uniform(key_list[5], (HEADS,), jnp.float32, -0.5, 0.5) * steps_of(key_list[5], (HEADS,), ((0, 4),), -0.4, 0.0), -0.5, 0.5)
    bypass_coefficients = jnp.clip(0.5 + 1.0 * jax.random.uniform(key_list[6], (HEADS,), jnp.float32) ** steps_of(key_list[6], (HEADS,), ((0, 4),), -0.2, 0.2), 0.5, 1.5)
    result_cotangent = draw_result_cotangent(jax.random.fold_in(key_list[8], 71), 0)
    return dict(head_inputs=head_inputs, entry_operator=entry_operator, memory_readout=memory_readout, unshifted_strides=unshifted_strides, log_decay_rates=log_decay_rates, stride_shift=stride_shift, bypass_coefficients=bypass_coefficients, result_cotangent=result_cotangent)


maximal_accuracy = lax.Precision.HIGHEST

def local_part(xg, write_operator, gram, dtr, rate_log, bias, skip):
    count = xg.shape[0]
    heads = dtr.shape[0]
    xg3 = xg.reshape(count, heads, -1)
    step = jax.nn.softplus(dtr + bias[:, None])
    logdecay = -jnp.exp(rate_log)[:, None] * step
    cum = jnp.cumsum(logdecay, axis=1)
    rows = lax.broadcasted_iota(jnp.int32, (count, count), 0)
    cols = lax.broadcasted_iota(jnp.int32, (count, count), 1)
    diff = cum[:, :, None] - cum[:, None, :]
    seg = jnp.exp(jnp.where((rows >= cols)[None], diff, -jnp.inf))
    weights = gram[None] * seg * step[:, None, :]
    inner = jnp.einsum('hts,shp->thp', weights, xg3, precision=maximal_accuracy)
    y_part = inner + skip[None, :, None] * xg3
    tail = jnp.exp(cum[:, -1:] - cum) * step
    scaled = xg3 * tail.T[:, :, None]
    state = jnp.einsum('shp,sn->hpn', scaled, write_operator, precision=maximal_accuracy)
    return (y_part, state, jnp.exp(cum))

def token_series(xs, bm, cm, dtr, log_decay_rates, stride_shift, bypass_coefficients):
    length = xs.shape[0]
    blocks = length // TOK_DEV
    heads = dtr.shape[0]
    xb = xs.reshape(blocks, TOK_DEV, heads * HEAD_DIM)
    bb = bm.reshape(blocks, TOK_DEV, -1)
    cb = cm.reshape(blocks, TOK_DEV, -1)
    db = dtr.reshape(heads, blocks, TOK_DEV).transpose(1, 0, 2)

    def block_step(carry, items):
        xblk, bblk, cblk, dblk = items
        gram = jnp.dot(cblk, bblk.T, precision=maximal_accuracy)
        y_part, state, growth_factor = local_part(xblk, bblk, gram, dblk, log_decay_rates, stride_shift, bypass_coefficients)
        readout = jnp.einsum('tn,hpn->thp', cblk, carry, precision=maximal_accuracy)
        yblk = y_part + growth_factor.T[:, :, None] * readout
        carry_next = growth_factor[:, -1][:, None, None] * carry + state
        return (carry_next, yblk)
    start = jnp.zeros((heads, HEAD_DIM, bm.shape[1]), jnp.float32)
    _, ys = lax.scan(block_step, start, (xb, bb, cb, db))
    return ys.reshape(length, heads * HEAD_DIM)

def forward(xf, brain_float_kind, cf, dtr, log_decay_rates, stride_shift, bypass_coefficients):

    def single(items):
        return token_series(items[0], items[1], items[2], items[3], log_decay_rates, stride_shift, bypass_coefficients)
    return lax.map(single, (xf, brain_float_kind, cf, dtr))

def reference(head_inputs, entry_operator, memory_readout, unshifted_strides, log_decay_rates, stride_shift, bypass_coefficients, result_cotangent):
    xf = head_inputs.astype(jnp.float32)
    brain_float_kind = entry_operator.astype(jnp.float32)
    cf = memory_readout.astype(jnp.float32)
    core, backward = jax.vjp(forward, xf, brain_float_kind, cf, unshifted_strides, log_decay_rates, stride_shift, bypass_coefficients)
    grads = backward(result_cotangent.astype(jnp.float32))
    return (core.astype(jnp.bfloat16), grads[0].astype(jnp.bfloat16), grads[1], grads[2], grads[3], grads[4], grads[5], grads[6])
```

```python
import functools

import jax
import jax.numpy as jnp
from jax import lax
from jax.experimental import pallas as pl
from jax.experimental.pallas import tpu as pltpu
from jax.sharding import PartitionSpec as P

F32, BF16 = jnp.float32, jnp.bfloat16
EXACT = lax.Precision.HIGHEST
NT = (((1,), (1,)), ((), ()))
NN = (((1,), (0,)), ((), ()))
LANES = 128
PAD = 8


def mm(a, b, dims=NN):
    return lax.dot_general(a, b, dims, preferred_element_type=F32)


def exact_mm(a, b, dims=NN):
    return lax.dot_general(a, b, dims, precision=EXACT, preferred_element_type=F32)


def split(v):
    hi = v.astype(BF16)
    return hi, (v - hi.astype(F32)).astype(BF16)


def spread(heads, width, first, lanes, rows=None):
    head = lax.broadcasted_iota(jnp.int32, (heads, lanes), 0)
    lane = lax.broadcasted_iota(jnp.int32, (heads, lanes), 1) + first
    inside = jnp.logical_and(lane >= head * width, lane < head * width + width)
    return jnp.where(inside, 1.0, 0.0).astype(BF16)


def expand(per_head, hot):
    hi, lo = split(per_head)
    return mm(jnp.concatenate([hi, lo], axis=1), jnp.concatenate([hot, hot], axis=0))


def scans(raw, par):
    rate, bias = par[:, 0:1], par[:, 1:2]
    z = raw + bias
    step = jnp.maximum(z, 0.0) + jnp.log1p(jnp.exp(-jnp.abs(z)))
    scale = -jnp.exp(rate)
    logdecay = scale * step
    count = raw.shape[1]
    early = lax.broadcasted_iota(jnp.int32, (count, count), 0)
    late = lax.broadcasted_iota(jnp.int32, (count, count), 1)
    upper = jnp.where(early <= late, 1.0, 0.0)
    cum = exact_mm(logdecay, upper)
    return z, step, scale, logdecay, cum, upper


def ends_kernel(c_ref, x_ref, g_ref, b_ref, r_ref, raw_ref, par_ref, own_ref, oth_ref, cum_ref, step_ref):
    heads, count = raw_ref.shape
    total = x_ref.shape[1]
    half = total // 2
    width = total // heads
    chunk = min(half, 512)
    _, step, _, _, cum, _ = scans(raw_ref[...], par_ref[...])
    cum_ref[...] = cum
    step_ref[...] = step
    tail = (jnp.exp(cum[:, -1:] - cum) * step).T
    grow = jnp.exp(cum).T
    bt = b_ref[...].astype(F32).T.astype(BF16)
    ct = r_ref[...].astype(F32).T.astype(BF16)
    bt2 = jnp.concatenate([bt, bt], axis=1)
    ct2 = jnp.concatenate([ct, ct], axis=1)
    c = c_ref[0]
    size = b_ref.shape[1]
    for which, out in ((c, own_ref), (1 - c, oth_ref)):
        for k in range(half // chunk):
            first = pl.multiple_of(which * half + k * chunk, chunk)
            hot = spread(heads, width, first, chunk)
            here = pl.ds(first, chunk)
            there = pl.ds(k * chunk, chunk)
            grow_x = expand(grow, hot)
            xt = expand(tail, hot) * x_ref[:, here].astype(F32)
            out[0, :size, there] = mm(bt2, jnp.concatenate(split(xt), axis=0))
            gt = grow_x * g_ref[:, here].astype(F32)
            out[1, :size, there] = mm(ct2, jnp.concatenate(split(gt), axis=0))
            last = jnp.broadcast_to(grow_x[count - 1 :, :], (PAD, chunk))
            out[0, size:, there] = last
            out[1, size:, there] = last


def inside_kernel(x_ref, g_ref, b_ref, r_ref, cum_ref, step_ref, inner_ref, dxin_ref, db_ref, dc_ref, cumt_ref, dgram_ref):
    heads, count = cum_ref.shape
    total = x_ref.shape[1]
    width = total // heads
    pack = LANES // width
    t_row = lax.broadcasted_iota(jnp.int32, (count, count), 0)
    t_col = lax.broadcasted_iota(jnp.int32, (count, count), 1)
    b, r = b_ref[...], r_ref[...]
    gram = jnp.where(t_row >= t_col, mm(r, b, NT), 0.0)
    gram_t = jnp.where(t_row <= t_col, mm(b, r, NT), 0.0)
    cum_all = cum_ref[...]
    cumt_ref[...] = jnp.concatenate([cum_all, jnp.zeros((LANES - heads, count), F32)], axis=0).T
    step_t = step_ref[...].T
    dgram_ref[...] = jnp.zeros_like(dgram_ref)
    lane = lax.broadcasted_iota(jnp.int32, (count, LANES), 1)

    def group(j, _):
        at = pl.multiple_of(j * LANES, LANES)
        x4 = x_ref[:, pl.ds(at, LANES)]
        g4 = g_ref[:, pl.ds(at, LANES)]
        cols = pltpu.roll(cumt_ref[...], LANES - j * pack, 1)
        his, los, thi, tlo, xs, gs = [], [], [], [], [], []
        dgram = dgram_ref[...]
        for i in range(pack):
            head = j * pack + i
            row = cum_ref[pl.ds(head, 1), :]
            step_row = step_ref[pl.ds(head, 1), :]
            diff = cols[:, i : i + 1] - row
            seg = jnp.exp(jnp.minimum(diff, 0.0)) * step_row
            seg_t = jnp.exp(jnp.minimum(-diff, 0.0))
            mine = jnp.logical_and(lane >= i * width, lane < (i + 1) * width)
            xm = jnp.where(mine, x4.astype(F32), 0.0).astype(BF16)
            gm = jnp.where(mine, g4.astype(F32), 0.0).astype(BF16)
            dgram = dgram + mm(gm, x4, NT) * seg
            hi, lo = split(gram * seg)
            his.append(hi)
            los.append(lo)
            hi, lo = split(gram_t * seg_t)
            thi.append(hi)
            tlo.append(lo)
            xs.append(xm)
            gs.append(gm)
        dgram_ref[...] = dgram
        inner_ref[:, pl.ds(at, LANES)] = mm(jnp.concatenate(his + los, axis=1), jnp.concatenate(xs + xs, axis=0))
        hot = spread(heads, width, at, LANES)
        back = mm(jnp.concatenate(thi + tlo, axis=1), jnp.concatenate(gs + gs, axis=0))
        dxin_ref[:, pl.ds(at, LANES)] = back * expand(step_t, hot)
        return 0

    lax.fori_loop(0, heads // pack, group, 0)
    dgram = jnp.where(t_row >= t_col, dgram_ref[...], 0.0)
    hi, lo = split(dgram)
    dc_ref[...] = mm(jnp.concatenate([hi, lo], axis=1), jnp.concatenate([b, b], axis=0))
    hi, lo = split(dgram.T)
    db_ref[...] = mm(jnp.concatenate([hi, lo], axis=1), jnp.concatenate([r, r], axis=0))


def after_kernel(
    c_ref, x_ref, g_ref, b_ref, r_ref, raw_ref, par_ref, inner_ref, dxin_ref, db0_ref, dc0_ref,
    own_ref, oth_ref, y_ref, dx_ref, db_ref, dc_ref, draw_ref, tot_ref,
):
    heads, count = raw_ref.shape
    total = x_ref.shape[1]
    half = total // 2
    width = total // heads
    chunk = min(half, 512)
    z, step, scale, logdecay, cum, upper = scans(raw_ref[...], par_ref[...])
    tail = (jnp.exp(cum[:, -1:] - cum) * step).T
    grow = jnp.exp(cum).T
    skip = jnp.broadcast_to(par_ref[:, 2:3], (heads, LANES)).T[:PAD]
    b, r = b_ref[...], r_ref[...]
    b2 = jnp.concatenate([b, b], axis=1)
    r2 = jnp.concatenate([r, r], axis=1)
    c = c_ref[0]
    db, dc = db0_ref[...], dc0_ref[...]
    uv = jnp.zeros((2 * count, heads), F32)
    sums = jnp.zeros((3 * PAD, heads), F32)
    for which, src in ((c, own_ref), (1 - c, oth_ref)):
        for k in range(half // chunk):
            first = pl.multiple_of(which * half + k * chunk, chunk)
            hot = spread(heads, width, first, chunk)
            here = pl.ds(first, chunk)
            there = pl.ds(k * chunk, chunk)
            x = x_ref[:, here].astype(F32)
            g = g_ref[:, here].astype(F32)
            grow_x, tail_x, skip_x = expand(grow, hot), expand(tail, hot), expand(skip, hot)[0:1]
            before, later = src[0, :, there], src[1, :, there]
            h_hi, h_lo = split(before)
            d_hi, d_lo = split(later)
            flow = inner_ref[:, here] + grow_x * mm(r2, jnp.concatenate([h_hi, h_lo], axis=0))
            y_ref[:, here] = (flow + skip_x * x).astype(BF16)
            reach = tail_x * mm(b2, jnp.concatenate([d_hi, d_lo], axis=0))
            back = dxin_ref[:, here] + reach
            dx_ref[:, here] = (back + skip_x * g).astype(BF16)
            uv_hi, uv_lo = split(jnp.concatenate([g * flow, x * back], axis=0))
            uv = uv + mm(uv_hi, hot, NT) + mm(uv_lo, hot, NT)
            parts = jnp.concatenate(
                [
                    jnp.sum((v).reshape(-1, PAD, chunk), axis=0)
                    for v in (x * reach, before * later, g * x)
                ],
                axis=0,
            )
            s_hi, s_lo = split(parts)
            sums = sums + mm(s_hi, hot, NT) + mm(s_lo, hot, NT)
            e_hi, e_lo = split(grow_x * g)
            dc = dc + mm(e_hi, h_hi, NT) + mm(e_hi, h_lo, NT) + mm(e_lo, h_hi, NT)
            t_hi, t_lo = split(tail_x * x)
            db = db + mm(t_hi, d_hi, NT) + mm(t_hi, d_lo, NT) + mm(t_lo, d_hi, NT)
    db_ref[...] = db
    dc_ref[...] = dc
    u = uv[:count].T
    v = uv[count:].T
    sums_t = sums.T
    reach_sum = jnp.sum(sums_t[:, :PAD], axis=1, keepdims=True)
    meet_sum = jnp.sum(sums_t[:, PAD : 2 * PAD], axis=1, keepdims=True)
    skip_sum = jnp.sum(sums_t[:, 2 * PAD :], axis=1, keepdims=True)
    end = reach_sum + jnp.exp(cum[:, -1:]) * meet_sum
    dlog = exact_mm(u - v, upper, NT) + end
    draw = (scale * dlog + v / step) * jax.nn.sigmoid(z)
    draw_ref[...] = draw
    column = lax.broadcasted_iota(jnp.int32, (heads, LANES), 1)
    rate_sum = jnp.sum(dlog * logdecay, axis=1, keepdims=True)
    bias_sum = jnp.sum(draw, axis=1, keepdims=True)
    tot_ref[...] = jnp.where(column == 0, rate_sum, jnp.where(column == 1, bias_sum, jnp.where(column == 2, skip_sum, 0.0)))


def call(kernel, outs, args, scratch=(), flops=0, scalar=False):
    vmem = pl.BlockSpec(memory_space=pltpu.VMEM)
    specs = [vmem] * len(args)
    if scalar:
        specs[0] = pl.BlockSpec(memory_space=pltpu.SMEM)
    size = sum(a.size * a.dtype.itemsize for a in (*args, *outs))
    return pl.pallas_call(
        kernel,
        out_shape=outs,
        in_specs=specs,
        out_specs=tuple([vmem] * len(outs)),
        scratch_shapes=list(scratch),
        cost_estimate=pl.CostEstimate(flops=flops, bytes_accessed=size, transcendentals=0),
        compiler_params=pltpu.CompilerParams(vmem_limit_bytes=48 << 20),
    )(*args)


def swap(value, axis, bit):
    return lax.ppermute(value, axis, [(i, i ^ bit) for i in range(lax.axis_size(axis))])


def gathered(value, axis):
    place, bit = lax.axis_index(axis), 1
    while bit < lax.axis_size(axis):
        other = swap(value, axis, bit)
        low = (place & bit) == 0
        value = jnp.concatenate([jnp.where(low, value, other), jnp.where(low, other, value)], axis=0)
        bit *= 2
    return value


def owned_sum(value, axis):
    place, bit = lax.axis_index(axis), lax.axis_size(axis) // 2
    while bit:
        lower, upper = jnp.split(value, 2, axis=0)
        low = (place & bit) == 0
        value = jnp.where(low, lower, upper) + swap(jnp.where(low, upper, lower), axis, bit)
        bit //= 2
    return value


def total_sum(value, axis):
    bit = 1
    while bit < lax.axis_size(axis):
        value = value + swap(value, axis, bit)
        bit *= 2
    return value


def chip_carries(total, size):
    n = lax.axis_size("ctx")
    place = lax.axis_index("ctx")
    zero = jnp.zeros_like(total[0, :size])

    def act(first, second, forward):
        if forward:
            return second[:size] + second[size : size + 1] * first[:size]
        return first[:size] + first[size : size + 1] * second[:size]

    if n == 8:
        x1, y1 = (place & 2) != 0, (place & 4) != 0
        from_y = swap(jnp.where(y1, total[1], total[0]), "ctx", 4)
        from_x = swap(jnp.where(x1, total[1], total[0]), "ctx", 2)
        far = swap(from_y, "ctx", 2)
        first, second = jnp.where(x1, far, from_y), jnp.where(x1, from_y, far)
        row = jnp.where(y1, act(first, second, True), act(first, second, False))
        ahead, behind = jnp.where(y1, row, zero), jnp.where(y1, zero, row)
        step = from_x[:size] + from_x[size : size + 1] * jnp.where(x1, ahead, behind)
        return jnp.where(x1, step, ahead), jnp.where(x1, behind, step)
    ahead, behind = zero, zero
    ahead_decay = behind_decay = jnp.ones_like(total[0, size : size + 1])
    fwd, bwd = total[0], total[1]
    bit = 2
    while bit < n:
        o_fwd, o_bwd = swap(fwd, "ctx", bit), swap(bwd, "ctx", bit)
        up = (place & bit) != 0
        ahead = jnp.where(up, ahead + ahead_decay * o_fwd[:size], ahead)
        ahead_decay = jnp.where(up, ahead_decay * o_fwd[size : size + 1], ahead_decay)
        behind = jnp.where(up, behind, behind + behind_decay * o_bwd[:size])
        behind_decay = jnp.where(up, behind_decay, behind_decay * o_bwd[size : size + 1])
        decay = fwd[size:] * o_fwd[size:]
        f1, f2 = jnp.where(up, o_fwd, fwd), jnp.where(up, fwd, o_fwd)
        b1, b2 = jnp.where(up, o_bwd, bwd), jnp.where(up, bwd, o_bwd)
        fwd = jnp.concatenate([act(f1, f2, True), decay], axis=0)
        bwd = jnp.concatenate([act(b1, b2, False), decay], axis=0)
        bit *= 2
    return ahead, behind


def local(x, b, r, raw, rate, bias, skip, g):
    x, b, r, raw, g = x[0], b[0], r[0], raw[0], g[0]
    heads, count = raw.shape
    total, size = x.shape[1], b.shape[1]
    half = total // 2
    par = gathered(jnp.stack([rate, bias, skip], axis=1), "dp")
    core = lax.axis_index("ctx") & 1
    odd = core == 1
    c = core.astype(jnp.int32).reshape(1)
    shape = jax.ShapeDtypeStruct
    message = shape((2, size + PAD, half), F32)
    small = shape((heads, count), F32)
    wide = shape((count, total), F32)
    square = shape((count, size), F32)
    own, oth, cum, step = call(
        ends_kernel, (message, message, small, small), (c, x, g, b, r, raw, par), flops=10**9, scalar=True
    )
    mate = swap(oth, "ctx", 1)
    s_o, g_o, a_o = own[0, :size], own[1, :size], own[0, size:]
    s_p, g_p, a_p = mate[0, :size], mate[1, :size], mate[0, size:]
    fwd = jnp.where(odd, a_o[0:1] * s_p + s_o, a_p[0:1] * s_o + s_p)
    bwd = jnp.where(odd, g_p + a_p[0:1] * g_o, g_o + a_o[0:1] * g_p)
    decay = a_o * a_p
    chip = jnp.stack([jnp.concatenate([fwd, decay], axis=0), jnp.concatenate([bwd, decay], axis=0)])
    ahead, behind = chip_carries(chip, size)
    inner, dxin, db0, dc0 = call(
        inside_kernel,
        (wide, wide, square, square),
        (x, g, b, r, cum, step),
        scratch=[pltpu.VMEM((count, LANES), F32), pltpu.VMEM((count, count), F32)],
        flops=10**9,
    )
    through = jnp.where(odd, a_p[0:1], a_o[0:1]) * ahead + jnp.where(odd, s_p, s_o)
    mine = jnp.where(odd, through, ahead), jnp.where(odd, behind, g_p + a_p[0:1] * behind)
    theirs = jnp.where(odd, ahead, through), jnp.where(odd, g_o + a_o[0:1] * behind, behind)
    mine, theirs = jnp.stack(mine), jnp.stack(theirs)
    rest = swap(theirs, "ctx", 1)
    outs = (shape((count, total), BF16), shape((count, total), BF16), square, square, small, shape((heads, LANES), F32))
    y, dx, db, dc, draw, tot = call(
        after_kernel, outs, (c, x, g, b, r, raw, par, inner, dxin, db0, dc0, mine, rest), flops=10**9, scalar=True
    )
    sums = owned_sum(total_sum(tot[:, :3], "ctx"), "dp")
    return (y[None], dx[None], db[None], dc[None], draw[None], sums[:, 0], sums[:, 1], sums[:, 2])


def solution(mesh):
    wide = P("dp", "ctx", None)
    strides = P("dp", None, "ctx")
    return jax.shard_map(
        local,
        mesh=mesh,
        in_specs=(wide, wide, wide, strides, P("dp"), P("dp"), P("dp"), wide),
        out_specs=(wide, wide, wide, wide, strides, P("dp"), P("dp"), P("dp")),
        check_vma=False,
    )
```

```python
import jax
import jax.numpy as jnp
from jax import lax
from jax.experimental import pallas as pl
from jax.experimental.pallas import tpu as pltpu
from jax.sharding import PartitionSpec as P


F32, BF16 = jnp.float32, jnp.bfloat16
EXACT = lax.Precision.HIGHEST
NT = (((1,), (1,)), ((), ()))
NN = (((1,), (0,)), ((), ()))
LANES = 128
PAD = 8


def mm(a, b, dims=NN):
    return lax.dot_general(a, b, dims, preferred_element_type=F32)


def exact_mm(a, b, dims=NN):
    return lax.dot_general(a, b, dims, precision=EXACT, preferred_element_type=F32)


def split(v):
    hi = v.astype(BF16)
    return hi, (v - hi.astype(F32)).astype(BF16)


def spread(heads, width, first, lanes):
    head = lax.broadcasted_iota(jnp.int32, (heads, lanes), 0)
    lane = lax.broadcasted_iota(jnp.int32, (heads, lanes), 1) + first
    inside = jnp.logical_and(lane >= head * width, lane < head * width + width)
    return jnp.where(inside, 1.0, 0.0).astype(BF16)


def expand(per_head, hot):
    hi, lo = split(per_head)
    return mm(jnp.concatenate([hi, lo], axis=1), jnp.concatenate([hot, hot], axis=0))


def scans(raw, par):
    rate, bias = par[:, 0:1], par[:, 1:2]
    z = raw + bias
    step = jnp.maximum(z, 0.0) + jnp.log1p(jnp.exp(-jnp.abs(z)))
    scale = -jnp.exp(rate)
    logdecay = scale * step
    count = raw.shape[1]
    early = lax.broadcasted_iota(jnp.int32, (count, count), 0)
    late = lax.broadcasted_iota(jnp.int32, (count, count), 1)
    upper = jnp.where(early <= late, 1.0, 0.0)
    cum = exact_mm(logdecay, upper)
    return z, step, scale, logdecay, cum, upper


def prep_kernel(x_ref, g_ref, b_ref, r_ref, raw_ref, *rest):
    outs, sems = rest[:5], rest[5]
    copies = [
        pltpu.make_async_copy(src, dst, sems.at[k])
        for k, (src, dst) in enumerate(zip((x_ref, g_ref, b_ref, r_ref, raw_ref), outs))
    ]
    for copy in copies:
        copy.start()
    for copy in copies:
        copy.wait()


def ends_kernel(c_ref, x_ref, g_ref, b_ref, r_ref, raw_ref, par_ref, own_ref, oth_ref, cum_ref, step_ref):
    heads, count = raw_ref.shape
    total = x_ref.shape[1]
    half = total // 2
    width = total // heads
    part = half // 2
    _, step, _, _, cum, _ = scans(raw_ref[...], par_ref[...])
    cum_ref[...] = cum
    step_ref[...] = step
    tail = (jnp.exp(cum[:, -1:] - cum) * step).T
    grow = jnp.exp(cum).T
    bt = b_ref[...].astype(F32).T.astype(BF16)
    ct = r_ref[...].astype(F32).T.astype(BF16)
    bt2 = jnp.concatenate([bt, bt], axis=1)
    ct2 = jnp.concatenate([ct, ct], axis=1)
    c = c_ref[0]
    size = b_ref.shape[1]
    for which, out in ((1 - c, oth_ref), (c, own_ref)):
        for k in range(2):
            first = pl.multiple_of(which * half + k * part, part)
            hot = spread(heads, width, first, part)
            here = pl.ds(first, part)
            grow_x = expand(grow, hot)
            xt = expand(tail, hot) * x_ref[:, here].astype(F32)
            out[0, k, :size] = mm(bt2, jnp.concatenate(split(xt), axis=0))
            gt = grow_x * g_ref[:, here].astype(F32)
            out[1, k, :size] = mm(ct2, jnp.concatenate(split(gt), axis=0))
            last = jnp.broadcast_to(grow_x[count - 1 :, :], (PAD, part))
            out[0, k, size:] = last
            out[1, k, size:] = last


def gram_kernel(b_ref, r_ref, gram_ref, gram_t_ref):
    b, r = b_ref[...], r_ref[...]
    row = lax.broadcasted_iota(jnp.int32, gram_ref.shape, 0)
    col = lax.broadcasted_iota(jnp.int32, gram_ref.shape, 1)
    gram_ref[...] = jnp.where(row >= col, mm(r, b, NT), 0.0)
    gram_t_ref[...] = jnp.where(row <= col, mm(b, r, NT), 0.0)


def inside_kernel(x_ref, g_ref, b_ref, r_ref, cum_ref, step_ref, gram_ref, gram_t_ref, inner_ref, dxin_ref, db_ref, dc_ref, cumt_ref, dgram_ref):
    heads, count = cum_ref.shape
    total = x_ref.shape[1]
    width = total // heads
    pack = LANES // width
    t_row = lax.broadcasted_iota(jnp.int32, (count, count), 0)
    t_col = lax.broadcasted_iota(jnp.int32, (count, count), 1)
    b, r = b_ref[...], r_ref[...]
    gram, gram_t = gram_ref[...], gram_t_ref[...]
    cum_all = cum_ref[...]
    cumt_ref[...] = jnp.concatenate([cum_all, jnp.zeros((LANES - heads, count), F32)], axis=0).T
    step_t = step_ref[...].T
    dgram_ref[...] = jnp.zeros_like(dgram_ref)
    lane = lax.broadcasted_iota(jnp.int32, (count, LANES), 1)

    def group(j, _):
        at = pl.multiple_of(j * LANES, LANES)
        x4 = x_ref[:, pl.ds(at, LANES)]
        g4 = g_ref[:, pl.ds(at, LANES)]
        cols = pltpu.roll(cumt_ref[...], LANES - j * pack, 1)
        his, los, thi, tlo, xs, gs = [], [], [], [], [], []
        dgram = dgram_ref[...]
        for i in range(pack):
            head = j * pack + i
            row = cum_ref[pl.ds(head, 1), :]
            step_row = step_ref[pl.ds(head, 1), :]
            diff = cols[:, i : i + 1] - row
            seg = jnp.exp(jnp.minimum(diff, 0.0)) * step_row
            seg_t = jnp.exp(jnp.minimum(-diff, 0.0))
            mine = jnp.logical_and(lane >= i * width, lane < (i + 1) * width)
            xm = jnp.where(mine, x4.astype(F32), 0.0).astype(BF16)
            gm = jnp.where(mine, g4.astype(F32), 0.0).astype(BF16)
            dgram = dgram + mm(gm, x4, NT) * seg
            hi, lo = split(gram * seg)
            his.append(hi)
            los.append(lo)
            hi, lo = split(gram_t * seg_t)
            thi.append(hi)
            tlo.append(lo)
            xs.append(xm)
            gs.append(gm)
        dgram_ref[...] = dgram
        inner_ref[:, pl.ds(at, LANES)] = mm(jnp.concatenate(his + los, axis=1), jnp.concatenate(xs + xs, axis=0))
        hot = spread(heads, width, at, LANES)
        back = mm(jnp.concatenate(thi + tlo, axis=1), jnp.concatenate(gs + gs, axis=0))
        dxin_ref[:, pl.ds(at, LANES)] = back * expand(step_t, hot)
        return 0

    lax.fori_loop(0, heads // pack, group, 0)
    dgram = jnp.where(t_row >= t_col, dgram_ref[...], 0.0)
    hi, lo = split(dgram)
    dc_ref[...] = mm(jnp.concatenate([hi, lo], axis=1), jnp.concatenate([b, b], axis=0))
    hi, lo = split(dgram.T)
    db_ref[...] = mm(jnp.concatenate([hi, lo], axis=1), jnp.concatenate([r, r], axis=0))


def carried(which, src, x_ref, g_ref, b_ref, r_ref, raw, par, inner_ref, dxin_ref, db, dc, uv, sums, y_ref, dx_ref, offset):
    heads, _ = raw.shape
    total = x_ref.shape[1]
    half = total // 2
    width = total // heads
    part = half // 2
    z, step, scale, logdecay, cum, upper = scans(raw, par)
    tail = (jnp.exp(cum[:, -1:] - cum) * step).T
    grow = jnp.exp(cum).T
    skip = jnp.broadcast_to(par[:, 2:3], (heads, LANES)).T[:PAD]
    b, r = b_ref[...], r_ref[...]
    b2 = jnp.concatenate([b, b], axis=1)
    r2 = jnp.concatenate([r, r], axis=1)
    for k in range(2):
        first = pl.multiple_of(which * half + k * part, part)
        hot = spread(heads, width, first, part)
        here = pl.ds(first, part)
        out = pl.ds(pl.multiple_of(offset + k * part, part), part)
        x = x_ref[:, here].astype(F32)
        g = g_ref[:, here].astype(F32)
        grow_x, tail_x, skip_x = expand(grow, hot), expand(tail, hot), expand(skip, hot)[0:1]
        before, later = src[0, k], src[1, k]
        h_hi, h_lo = split(before)
        d_hi, d_lo = split(later)
        flow = inner_ref[:, here] + grow_x * mm(r2, jnp.concatenate([h_hi, h_lo], axis=0))
        y_ref[:, out] = (flow + skip_x * x).astype(BF16)
        reach = tail_x * mm(b2, jnp.concatenate([d_hi, d_lo], axis=0))
        back = dxin_ref[:, here] + reach
        dx_ref[:, out] = (back + skip_x * g).astype(BF16)
        uv_hi, uv_lo = split(jnp.concatenate([g * flow, x * back], axis=0))
        uv = uv + mm(uv_hi, hot, NT) + mm(uv_lo, hot, NT)
        parts = jnp.concatenate(
            [jnp.sum(v.reshape(-1, PAD, part), axis=0) for v in (x * reach, before * later, g * x)], axis=0
        )
        s_hi, s_lo = split(parts)
        sums = sums + mm(s_hi, hot, NT) + mm(s_lo, hot, NT)
        e_hi, e_lo = split(grow_x * g)
        dc = dc + mm(e_hi, h_hi, NT) + mm(e_hi, h_lo, NT) + mm(e_lo, h_hi, NT)
        t_hi, t_lo = split(tail_x * x)
        db = db + mm(t_hi, d_hi, NT) + mm(t_hi, d_lo, NT) + mm(t_lo, d_hi, NT)
    return db, dc, uv, sums, (z, step, scale, logdecay, cum, upper)


def first_kernel(
    c_ref, x_ref, g_ref, b_ref, r_ref, raw_ref, par_ref, inner_ref, dxin_ref, db0_ref, dc0_ref, src_ref,
    y_ref, dx_ref, db_ref, dc_ref, uv_ref, sums_ref,
):
    uv, sums = jnp.zeros(uv_ref.shape, F32), jnp.zeros(sums_ref.shape, F32)
    db_ref[...], dc_ref[...], uv_ref[...], sums_ref[...], _ = carried(
        c_ref[0], src_ref, x_ref, g_ref, b_ref, r_ref, raw_ref[...], par_ref[...], inner_ref, dxin_ref,
        db0_ref[...], dc0_ref[...], uv, sums, y_ref, dx_ref, 0,
    )


def second_kernel(
    c_ref, x_ref, g_ref, b_ref, r_ref, raw_ref, par_ref, inner_ref, dxin_ref, db0_ref, dc0_ref, src_ref,
    y0_ref, dx0_ref, uv0_ref, sums0_ref, y_ref, dx_ref, db_ref, dc_ref, draw_ref, tot_ref,
):
    heads, count = raw_ref.shape
    half = x_ref.shape[1] // 2
    c = c_ref[0]
    other = (1 - c) * half
    db_ref[...], dc_ref[...], uv, sums, (z, step, scale, logdecay, cum, upper) = carried(
        1 - c, src_ref, x_ref, g_ref, b_ref, r_ref, raw_ref[...], par_ref[...], inner_ref, dxin_ref,
        db0_ref[...], dc0_ref[...], uv0_ref[...], sums0_ref[...], y_ref, dx_ref, other,
    )
    mine = pl.ds(pl.multiple_of(c * half, half), half)
    y_ref[:, mine] = y0_ref[...]
    dx_ref[:, mine] = dx0_ref[...]
    u = uv[:count].T
    v = uv[count:].T
    sums_t = sums.T
    reach_sum = jnp.sum(sums_t[:, :PAD], axis=1, keepdims=True)
    meet_sum = jnp.sum(sums_t[:, PAD : 2 * PAD], axis=1, keepdims=True)
    skip_sum = jnp.sum(sums_t[:, 2 * PAD :], axis=1, keepdims=True)
    end = reach_sum + jnp.exp(cum[:, -1:]) * meet_sum
    dlog = exact_mm(u - v, upper, NT) + end
    draw = (scale * dlog + v / step) * jax.nn.sigmoid(z)
    draw_ref[...] = draw
    column = lax.broadcasted_iota(jnp.int32, (heads, LANES), 1)
    rate_sum = jnp.sum(dlog * logdecay, axis=1, keepdims=True)
    bias_sum = jnp.sum(draw, axis=1, keepdims=True)
    tot_ref[...] = jnp.where(column == 0, rate_sum, jnp.where(column == 1, bias_sum, jnp.where(column == 2, skip_sum, 0.0)))


def call(kernel, outs, args, scratch=(), flops=0, scalar=False, off_chip=False):
    if off_chip:
        args = tuple(pltpu.with_memory_space_constraint(a, pltpu.HBM) for a in args)
    vmem = pl.BlockSpec(memory_space=pltpu.VMEM)
    specs = [pl.BlockSpec(memory_space=pltpu.HBM) if off_chip else vmem] * len(args)
    if scalar:
        specs[0] = pl.BlockSpec(memory_space=pltpu.SMEM)
    size = sum(a.size * a.dtype.itemsize for a in (*args, *outs))
    return pl.pallas_call(
        kernel,
        out_shape=outs,
        in_specs=specs,
        out_specs=tuple([vmem] * len(outs)),
        scratch_shapes=list(scratch),
        cost_estimate=pl.CostEstimate(flops=flops, bytes_accessed=size, transcendentals=0),
        compiler_params=pltpu.CompilerParams(vmem_limit_bytes=32 << 20),
    )(*args)


def swap(value, axis, bit):
    return lax.ppermute(value, axis, [(i, i ^ bit) for i in range(lax.axis_size(axis))])


def gathered(value, axis):
    place, bit = lax.axis_index(axis), 1
    while bit < lax.axis_size(axis):
        other = swap(value, axis, bit)
        low = (place & bit) == 0
        value = jnp.concatenate([jnp.where(low, value, other), jnp.where(low, other, value)], axis=0)
        bit *= 2
    return value


def owned_sum(value, axis):
    place, bit = lax.axis_index(axis), lax.axis_size(axis) // 2
    while bit:
        lower, upper = jnp.split(value, 2, axis=0)
        low = (place & bit) == 0
        value = jnp.where(low, lower, upper) + swap(jnp.where(low, upper, lower), axis, bit)
        bit //= 2
    return value


def total_sum(value, axis):
    bit = 1
    while bit < lax.axis_size(axis):
        value = value + swap(value, axis, bit)
        bit *= 2
    return value


def planned(mesh_size):
    return mesh_size == 8


def chip_carries(total, size):
    n = lax.axis_size("ctx")
    place = lax.axis_index("ctx")

    def state(v):
        return v[..., :size, :]

    def decay(v):
        return v[..., size : size + 1, :]

    if planned(n):
        x1, y1 = (place & 2) != 0, (place & 4) != 0
        bent = x1 != y1
        (f_a, f_b), (r_a, r_b) = total[0], total[1]
        own_a, own_b = jnp.where(y1, r_a, f_a), jnp.where(y1, f_b, r_b)
        xa = swap(own_a, "ctx", 2)
        yb = swap(jnp.where(y1, r_b, f_b), "ctx", 4)
        late = swap(jnp.where(y1, jnp.where(x1, r_b, f_a), jnp.where(x1, r_a, f_b)), "ctx", 2)
        diag = swap(f_b[size:], "ctx", 6)
        first, second = jnp.where(x1, xa, own_a), jnp.where(x1, own_a, xa)
        row = jnp.where(y1, state(first) + decay(first) * state(second), state(second) + decay(second) * state(first))
        ya = swap(row, "ctx", 4)
        both = state(own_b) + decay(own_b) * diag[:1] * state(yb)
        onward = jnp.concatenate([jnp.where(bent, both, state(yb)), jnp.where(bent, own_b[size:], yb[size:])], axis=0)
        xb = swap(onward, "ctx", 2)
        far = jnp.stack([jnp.where(bent, ya, state(late) + decay(late) * ya), state(xb) + decay(xb) * state(yb)])
        near = jnp.where(bent, jnp.stack([state(xa), state(late)]), 0.0)
        return jnp.where(y1, far, near), jnp.where(y1, near, far)
    fwd, bwd = total[0], total[1]
    ahead = behind = jnp.zeros_like(state(fwd))
    ahead_decay = behind_decay = jnp.ones_like(decay(fwd))
    bit = 2
    while bit < n:
        o_fwd, o_bwd = swap(fwd, "ctx", bit), swap(bwd, "ctx", bit)
        up = (place & bit) != 0
        ahead = jnp.where(up, ahead + ahead_decay * state(o_fwd), ahead)
        ahead_decay = jnp.where(up, ahead_decay * decay(o_fwd), ahead_decay)
        behind = jnp.where(up, behind, behind + behind_decay * state(o_bwd))
        behind_decay = jnp.where(up, behind_decay, behind_decay * decay(o_bwd))
        both = fwd[..., size:, :] * o_fwd[..., size:, :]
        f1, f2 = jnp.where(up, o_fwd, fwd), jnp.where(up, fwd, o_fwd)
        b1, b2 = jnp.where(up, o_bwd, bwd), jnp.where(up, bwd, o_bwd)
        fwd = jnp.concatenate([state(f2) + decay(f2) * state(f1), both], axis=-2)
        bwd = jnp.concatenate([state(b1) + decay(b1) * state(b2), both], axis=-2)
        bit *= 2
    return ahead, behind


def local(x, b, r, raw, rate, bias, skip, g):
    return layer(x[0], b[0], r[0], raw[0], rate, bias, skip, g[0])


def layer(x, b, r, raw, rate, bias, skip, g):
    heads, count = raw.shape
    total, size = x.shape[1], b.shape[1]
    half = total // 2
    part = half // 2
    shape = jax.ShapeDtypeStruct
    par = gathered(jnp.stack([rate, bias, skip], axis=1), "dp")
    core = lax.axis_index("ctx") & 1
    odd = core == 1
    c = core.astype(jnp.int32).reshape(1)
    message = shape((2, 2, size + PAD, part), F32)
    small = shape((heads, count), F32)
    wide = shape((count, total), F32)
    square = shape((count, size), F32)
    mixed = shape((count, count), F32)
    args = (x, g, b, r, raw)
    x, g, b, r, raw = call(
        prep_kernel, tuple(shape(v.shape, v.dtype) for v in args), args,
        scratch=[pltpu.SemaphoreType.DMA((len(args),))], off_chip=True,
    )
    own, oth, cum, step = call(
        ends_kernel, (message, message, small, small), (c, x, g, b, r, raw, par), flops=10**9, scalar=True
    )
    mate = swap(oth, "ctx", 1)
    s_o, g_o, a_o = own[0, :, :size], own[1, :, :size], own[0, :, size:]
    s_p, g_p, a_p = mate[0, :, :size], mate[1, :, :size], mate[0, :, size:]
    fwd = jnp.where(odd, a_o[:, :1] * s_p + s_o, a_p[:, :1] * s_o + s_p)
    bwd = jnp.where(odd, g_p + a_p[:, :1] * g_o, g_o + a_o[:, :1] * g_p)
    decay = a_o * a_p
    chip = jnp.stack([jnp.concatenate([fwd, decay], axis=1), jnp.concatenate([bwd, decay], axis=1)])
    ahead, behind = chip_carries(chip, size)
    gram, gram_t = call(gram_kernel, (mixed, mixed), (b, r), flops=10**7)
    inner, dxin, db0, dc0 = call(
        inside_kernel,
        (wide, wide, square, square),
        (x, g, b, r, cum, step, gram, gram_t),
        scratch=[pltpu.VMEM((count, LANES), F32), pltpu.VMEM((count, count), F32)],
        flops=10**9,
    )
    through = jnp.where(odd, a_p[:, :1], a_o[:, :1]) * ahead + jnp.where(odd, s_p, s_o)
    theirs = jnp.where(odd, ahead, through), jnp.where(odd, g_o + a_o[:, :1] * behind, behind)
    rest = swap(jnp.stack(theirs), "ctx", 1)
    mine = jnp.stack([jnp.where(odd, through, ahead), jnp.where(odd, behind, g_p + a_p[:, :1] * behind)])
    ready = (c, x, g, b, r, raw, par, inner, dxin)
    halved = shape((count, half), BF16)
    whole = shape((count, total), BF16)
    y0, dx0, db1, dc1, uv, sums = call(
        first_kernel,
        (halved, halved, square, square, shape((2 * count, heads), F32), shape((3 * PAD, heads), F32)),
        (*ready, db0, dc0, mine), flops=10**9, scalar=True,
    )
    y, dx, db, dc, draw, tot = call(
        second_kernel, (whole, whole, square, square, small, shape((heads, LANES), F32)),
        (*ready, db1, dc1, rest, y0, dx0, uv, sums), flops=10**9, scalar=True,
    )
    owned = owned_sum(total_sum(tot[:, :3], "ctx"), "dp")
    return (y[None], dx[None], db[None], dc[None], draw[None], owned[:, 0], owned[:, 1], owned[:, 2])


def solution(mesh):
    wide = P("dp", "ctx", None)
    strides = P("dp", None, "ctx")
    return jax.shard_map(
        local,
        mesh=mesh,
        in_specs=(wide, wide, wide, strides, P("dp"), P("dp"), P("dp"), wide),
        out_specs=(wide, wide, wide, wide, strides, P("dp"), P("dp"), P("dp")),
        check_vma=False,
    )
```

```python
import functools

import jax
import jax.numpy as jnp
from jax import lax
from jax.experimental import pallas as pl
from jax.experimental.pallas import tpu as pltpu
from jax.sharding import PartitionSpec as P


F32, BF16 = jnp.float32, jnp.bfloat16
EXACT = lax.Precision.HIGHEST
NT = (((1,), (1,)), ((), ()))
NN = (((1,), (0,)), ((), ()))
LANES = 128
PAD = 8


def mm(a, b, dims=NN):
    return lax.dot_general(a, b, dims, preferred_element_type=F32)


def exact_mm(a, b, dims=NN):
    return lax.dot_general(a, b, dims, precision=EXACT, preferred_element_type=F32)


def split(v):
    hi = v.astype(BF16)
    return hi, (v - hi.astype(F32)).astype(BF16)


def spread(heads, width, first, lanes):
    head = lax.broadcasted_iota(jnp.int32, (heads, lanes), 0)
    lane = lax.broadcasted_iota(jnp.int32, (heads, lanes), 1) + first
    inside = jnp.logical_and(lane >= head * width, lane < head * width + width)
    return jnp.where(inside, 1.0, 0.0).astype(BF16)


def expand(per_head, hot):
    hi, lo = split(per_head)
    return mm(jnp.concatenate([hi, lo], axis=1), jnp.concatenate([hot, hot], axis=0))


def relative(n, place, block, src_ref, dst_ref):
    for i in range(n):
        dst_ref[pl.ds(i * block, block), :] = src_ref[pl.ds(pl.multiple_of((place ^ i) * block, block), block), :]


def scans(raw, par):
    rate, bias = par[:, 0:1], par[:, 1:2]
    z = raw + bias
    step = jnp.maximum(z, 0.0) + jnp.log1p(jnp.exp(-jnp.abs(z)))
    scale = -jnp.exp(rate)
    logdecay = scale * step
    count = raw.shape[1]
    early = lax.broadcasted_iota(jnp.int32, (count, count), 0)
    late = lax.broadcasted_iota(jnp.int32, (count, count), 1)
    upper = jnp.where(early <= late, 1.0, 0.0)
    cum = exact_mm(logdecay, upper)
    return z, step, scale, logdecay, cum, upper


def prep_kernel(x_ref, g_ref, b_ref, r_ref, raw_ref, *rest):
    outs, sems = rest[:5], rest[5]
    copies = [
        pltpu.make_async_copy(src, dst, sems.at[k])
        for k, (src, dst) in enumerate(zip((x_ref, g_ref, b_ref, r_ref, raw_ref), outs))
    ]
    for copy in copies:
        copy.start()
    for copy in copies:
        copy.wait()


def ends_kernel(
    groups, place_ref, x_ref, g_ref, b_ref, r_ref, raw_ref, got_ref, own_ref, oth_ref, cum_ref, step_ref, par_ref, mixed_ref,
):
    heads, count = raw_ref.shape
    rows = got_ref.shape[0]
    mixed_ref[...] = jnp.concatenate([got_ref[...], jnp.zeros((LANES - rows, heads), F32)], axis=0).T
    relative(groups, place_ref[1], heads // groups, mixed_ref, par_ref)
    total = x_ref.shape[1]
    half = total // 2
    width = total // heads
    part = half // 2
    _, step, _, _, cum, _ = scans(raw_ref[...], par_ref[...])
    cum_ref[...] = cum
    step_ref[...] = step
    tail = (jnp.exp(cum[:, -1:] - cum) * step).T
    grow = jnp.exp(cum).T
    bt = b_ref[...].astype(F32).T.astype(BF16)
    ct = r_ref[...].astype(F32).T.astype(BF16)
    bt2 = jnp.concatenate([bt, bt], axis=1)
    ct2 = jnp.concatenate([ct, ct], axis=1)
    c = place_ref[0] & 1
    size = b_ref.shape[1]
    for which, out in ((1 - c, oth_ref), (c, own_ref)):
        for k in range(2):
            first = pl.multiple_of(which * half + k * part, part)
            hot = spread(heads, width, first, part)
            here = pl.ds(first, part)
            grow_x = expand(grow, hot)
            xt = expand(tail, hot) * x_ref[:, here].astype(F32)
            out[0, k, :size] = mm(bt2, jnp.concatenate(split(xt), axis=0))
            gt = grow_x * g_ref[:, here].astype(F32)
            out[1, k, :size] = mm(ct2, jnp.concatenate(split(gt), axis=0))
            last = jnp.broadcast_to(grow_x[count - 1 :, :], (PAD, part))
            out[0, k, size:] = last
            out[1, k, size:] = last


def gram_kernel(b_ref, r_ref, gram_ref, gram_t_ref):
    b, r = b_ref[...], r_ref[...]
    row = lax.broadcasted_iota(jnp.int32, gram_ref.shape, 0)
    col = lax.broadcasted_iota(jnp.int32, gram_ref.shape, 1)
    gram_ref[...] = jnp.where(row >= col, mm(r, b, NT), 0.0)
    gram_t_ref[...] = jnp.where(row <= col, mm(b, r, NT), 0.0)


def totals_kernel(place_ref, own_ref, mate_ref, xa_ref, yb_ref, late_ref, diag_ref, kept_ref):
    place = place_ref[0]
    odd, x1, y1 = (place & 1) != 0, (place >> 1) & 1, (place >> 2) & 1
    size = own_ref.shape[2] - PAD

    def total(way, part, first, second, out):
        f, l = first[way, part, :size], second[way, part, :size]
        fd, ld = first[way, part, size:], second[way, part, size:]
        lead = jnp.broadcast_to((way == 0).astype(F32), fd[:1].shape)
        keep = jnp.where(lead > 0.0, ld[:1], 1.0)
        onto = jnp.where(lead > 0.0, 1.0, fd[:1])
        out[:size] = keep * f + onto * l
        out[size:] = fd * ld

    def all_totals(first, second):
        total(y1, 0, first, second, xa_ref)
        total(y1, 1, first, second, yb_ref)
        total(1 - y1, 1, first, second, kept_ref)

        @pl.when(x1 != y1)
        def _():
            total(1 - y1, 0, first, second, late_ref)

        @pl.when(x1 == y1)
        def _():
            late_ref[...] = yb_ref[...]

        diag_ref[...] = kept_ref[size:]

    @pl.when(odd)
    def _():
        all_totals(mate_ref, own_ref)

    @pl.when(jnp.logical_not(odd))
    def _():
        all_totals(own_ref, mate_ref)


def row_kernel(place_ref, sent_ref, xa_ref, row_ref):
    place = place_ref[0]
    x1, y1 = (place >> 1) & 1, (place >> 2) & 1
    size = row_ref.shape[0]

    @pl.when(x1 != y1)
    def _():
        row_ref[...] = sent_ref[:size] + sent_ref[size : size + 1] * xa_ref[:size]

    @pl.when(x1 == y1)
    def _():
        row_ref[...] = xa_ref[:size] + xa_ref[size : size + 1] * sent_ref[:size]


def onward_kernel(place_ref, kept_ref, diag_ref, yb_ref, xb_ref):
    place = place_ref[0]
    x1, y1 = (place >> 1) & 1, (place >> 2) & 1
    size = xb_ref.shape[0] - PAD

    @pl.when(x1 != y1)
    def _():
        xb_ref[:size] = kept_ref[:size] + kept_ref[size : size + 1] * diag_ref[:1] * yb_ref[:size]
        xb_ref[size:] = kept_ref[size:]

    @pl.when(x1 == y1)
    def _():
        xb_ref[...] = yb_ref[...]


def reach_kernel(place_ref, own_ref, mate_ref, xa_ref, yb_ref, late_ref, ya_ref, xb_ref, mine_ref, rest_ref):
    place = place_ref[0]
    odd, x1, y1 = (place & 1) != 0, (place >> 1) & 1, (place >> 2) & 1
    size = ya_ref.shape[0]

    def spread_to(first, second, to_first, to_second):
        for part in range(2):
            if part == 0:
                bent_far, near = ya_ref[...], xa_ref
                flat_far = late_ref[:size] + late_ref[size : size + 1] * ya_ref[...]
                far = jnp.where(jnp.broadcast_to(x1 != y1, flat_far.shape), bent_far, flat_far)
            else:
                near = late_ref
                far = xb_ref[:size] + xb_ref[size : size + 1] * yb_ref[:size]
            near = jnp.where(jnp.broadcast_to(x1 != y1, far.shape), near[:size], 0.0)
            forward = jnp.broadcast_to(y1 == 1, far.shape)
            ahead, behind = jnp.where(forward, far, near), jnp.where(forward, near, far)
            to_first[0, part] = ahead
            to_second[0, part] = first[0, part, size : size + 1] * ahead + first[0, part, :size]
            to_second[1, part] = behind
            to_first[1, part] = second[1, part, size : size + 1] * behind + second[1, part, :size]

    @pl.when(odd)
    def _():
        spread_to(mate_ref, own_ref, rest_ref, mine_ref)

    @pl.when(jnp.logical_not(odd))
    def _():
        spread_to(own_ref, mate_ref, mine_ref, rest_ref)


def inside_kernel(x_ref, g_ref, b_ref, r_ref, cum_ref, step_ref, gram_ref, gram_t_ref, inner_ref, dxin_ref, db_ref, dc_ref, cumt_ref, dgram_ref):
    heads, count = cum_ref.shape
    total = x_ref.shape[1]
    width = total // heads
    pack = LANES // width
    t_row = lax.broadcasted_iota(jnp.int32, (count, count), 0)
    t_col = lax.broadcasted_iota(jnp.int32, (count, count), 1)
    b, r = b_ref[...], r_ref[...]
    gram, gram_t = gram_ref[...], gram_t_ref[...]
    cum_all = cum_ref[...]
    cumt_ref[...] = jnp.concatenate([cum_all, jnp.zeros((LANES - heads, count), F32)], axis=0).T
    step_t = step_ref[...].T
    dgram_ref[...] = jnp.zeros_like(dgram_ref)
    lane = lax.broadcasted_iota(jnp.int32, (count, LANES), 1)

    def group(j, _):
        at = pl.multiple_of(j * LANES, LANES)
        x4 = x_ref[:, pl.ds(at, LANES)]
        g4 = g_ref[:, pl.ds(at, LANES)]
        cols = pltpu.roll(cumt_ref[...], LANES - j * pack, 1)
        his, los, thi, tlo, xs, gs = [], [], [], [], [], []
        dgram = dgram_ref[...]
        for i in range(pack):
            head = j * pack + i
            row = cum_ref[pl.ds(head, 1), :]
            step_row = step_ref[pl.ds(head, 1), :]
            diff = cols[:, i : i + 1] - row
            seg = jnp.exp(jnp.minimum(diff, 0.0)) * step_row
            seg_t = jnp.exp(jnp.minimum(-diff, 0.0))
            mine = jnp.logical_and(lane >= i * width, lane < (i + 1) * width)
            xm = jnp.where(mine, x4.astype(F32), 0.0).astype(BF16)
            gm = jnp.where(mine, g4.astype(F32), 0.0).astype(BF16)
            dgram = dgram + mm(gm, x4, NT) * seg
            hi, lo = split(gram * seg)
            his.append(hi)
            los.append(lo)
            hi, lo = split(gram_t * seg_t)
            thi.append(hi)
            tlo.append(lo)
            xs.append(xm)
            gs.append(gm)
        dgram_ref[...] = dgram
        inner_ref[:, pl.ds(at, LANES)] = mm(jnp.concatenate(his + los, axis=1), jnp.concatenate(xs + xs, axis=0))
        hot = spread(heads, width, at, LANES)
        back = mm(jnp.concatenate(thi + tlo, axis=1), jnp.concatenate(gs + gs, axis=0))
        dxin_ref[:, pl.ds(at, LANES)] = back * expand(step_t, hot)
        return 0

    lax.fori_loop(0, heads // pack, group, 0)
    dgram = jnp.where(t_row >= t_col, dgram_ref[...], 0.0)
    hi, lo = split(dgram)
    dc_ref[...] = mm(jnp.concatenate([hi, lo], axis=1), jnp.concatenate([b, b], axis=0))
    hi, lo = split(dgram.T)
    db_ref[...] = mm(jnp.concatenate([hi, lo], axis=1), jnp.concatenate([r, r], axis=0))


def lanes_of(heads, total, which):
    half = total // 2
    part = half // 2
    for k in range(2):
        first = pl.multiple_of(which * half + k * part, part)
        yield k, pl.ds(first, part), pl.ds(k * part, part), spread(heads, total // heads, first, part)


def carried(which, src, x_ref, g_ref, b_ref, r_ref, raw, par, inner_ref, dxin_ref, uv, sums, y_ref, dx_ref):
    heads, _ = raw.shape
    scanned = scans(raw, par)
    _, step, _, _, cum, _ = scanned
    tail = (jnp.exp(cum[:, -1:] - cum) * step).T
    grow = jnp.exp(cum).T
    skip = jnp.broadcast_to(par[:, 2:3], (heads, LANES)).T[:PAD]
    b, r = b_ref[...], r_ref[...]
    b2 = jnp.concatenate([b, b], axis=1)
    r2 = jnp.concatenate([r, r], axis=1)
    for k, here, out, hot in lanes_of(heads, x_ref.shape[1], which):
        x = x_ref[:, here].astype(F32)
        g = g_ref[:, here].astype(F32)
        grow_x, tail_x, skip_x = expand(grow, hot), expand(tail, hot), expand(skip, hot)[0:1]
        before, later = src[0, k], src[1, k]
        flow = inner_ref[:, here] + grow_x * mm(r2, jnp.concatenate(split(before), axis=0))
        y_ref[:, out] = (flow + skip_x * x).astype(BF16)
        reach = tail_x * mm(b2, jnp.concatenate(split(later), axis=0))
        back = dxin_ref[:, here] + reach
        dx_ref[:, out] = (back + skip_x * g).astype(BF16)
        uv_hi, uv_lo = split(jnp.concatenate([g * flow, x * back], axis=0))
        uv = uv + mm(uv_hi, hot, NT) + mm(uv_lo, hot, NT)
        parts = jnp.concatenate(
            [jnp.sum(v.reshape(-1, PAD, v.shape[1]), axis=0) for v in (x * reach, before * later, g * x)], axis=0
        )
        s_hi, s_lo = split(parts)
        sums = sums + mm(s_hi, hot, NT) + mm(s_lo, hot, NT)
    return uv, sums, scanned


def projected(which, src, x_ref, g_ref, cum, step, db, dc):
    tail = (jnp.exp(cum[:, -1:] - cum) * step).T
    grow = jnp.exp(cum).T
    for k, here, _, hot in lanes_of(cum.shape[0], x_ref.shape[1], which):
        h_hi, h_lo = split(src[0, k])
        d_hi, d_lo = split(src[1, k])
        e_hi, e_lo = split(expand(grow, hot) * g_ref[:, here].astype(F32))
        dc = dc + mm(e_hi, h_hi, NT) + mm(e_hi, h_lo, NT) + mm(e_lo, h_hi, NT)
        t_hi, t_lo = split(expand(tail, hot) * x_ref[:, here].astype(F32))
        db = db + mm(t_hi, d_hi, NT) + mm(t_hi, d_lo, NT) + mm(t_lo, d_hi, NT)
    return db, dc


def first_kernel(
    place_ref, x_ref, g_ref, b_ref, r_ref, raw_ref, par_ref, inner_ref, dxin_ref, src_ref, cum_ref, step_ref,
    db0_ref, dc0_ref, y_ref, dx_ref, uv_ref, sums_ref, db_ref, dc_ref,
):
    c = place_ref[0] & 1
    uv, sums = jnp.zeros(uv_ref.shape, F32), jnp.zeros(sums_ref.shape, F32)
    uv_ref[...], sums_ref[...], _ = carried(
        c, src_ref, x_ref, g_ref, b_ref, r_ref, raw_ref[...], par_ref[...], inner_ref, dxin_ref, uv, sums, y_ref, dx_ref
    )
    db_ref[...], dc_ref[...] = projected(
        c, src_ref, x_ref, g_ref, cum_ref[...], step_ref[...], db0_ref[...], dc0_ref[...]
    )


def second_kernel(
    groups, place_ref, x_ref, g_ref, b_ref, r_ref, raw_ref, par_ref, inner_ref, dxin_ref, src_ref,
    uv0_ref, sums0_ref, y_ref, dx_ref, draw_ref, tot_ref, col_ref, rel_ref,
):
    heads, count = raw_ref.shape
    other = 1 - (place_ref[0] & 1)
    uv, sums, (z, step, scale, logdecay, cum, upper) = carried(
        other, src_ref, x_ref, g_ref, b_ref, r_ref, raw_ref[...], par_ref[...], inner_ref, dxin_ref,
        uv0_ref[...], sums0_ref[...], y_ref, dx_ref,
    )
    u = uv[:count].T
    v = uv[count:].T
    sums_t = sums.T
    reach_sum = jnp.sum(sums_t[:, :PAD], axis=1, keepdims=True)
    meet_sum = jnp.sum(sums_t[:, PAD : 2 * PAD], axis=1, keepdims=True)
    skip_sum = jnp.sum(sums_t[:, 2 * PAD :], axis=1, keepdims=True)
    end = reach_sum + jnp.exp(cum[:, -1:]) * meet_sum
    dlog = exact_mm(u - v, upper, NT) + end
    draw = (scale * dlog + v / step) * jax.nn.sigmoid(z)
    draw_ref[...] = draw
    column = lax.broadcasted_iota(jnp.int32, (heads, LANES), 1)
    rate_sum = jnp.sum(dlog * logdecay, axis=1, keepdims=True)
    bias_sum = jnp.sum(draw, axis=1, keepdims=True)
    col_ref[...] = jnp.where(column == 0, rate_sum, jnp.where(column == 1, bias_sum, jnp.where(column == 2, skip_sum, 0.0)))
    relative(groups, place_ref[1], heads // groups, col_ref, rel_ref)
    tot_ref[...] = rel_ref[...].T[:PAD]


def third_kernel(
    place_ref, x_ref, g_ref, cum_ref, step_ref, src_ref, db0_ref, dc0_ref, y0_ref, dx0_ref, y1_ref, dx1_ref,
    y_ref, dx_ref, db_ref, dc_ref,
):
    c = place_ref[0] & 1
    half = x_ref.shape[1] // 2
    for which, ys, dxs in ((c, y0_ref, dx0_ref), (1 - c, y1_ref, dx1_ref)):
        at = pl.ds(pl.multiple_of(which * half, half), half)
        y_ref[:, at] = ys[...]
        dx_ref[:, at] = dxs[...]
    db_ref[...], dc_ref[...] = projected(
        1 - c, src_ref, x_ref, g_ref, cum_ref[...], step_ref[...], db0_ref[...], dc0_ref[...]
    )


def call(kernel, outs, args, scratch=(), flops=0, scalar=False, off_chip=False):
    if off_chip:
        args = tuple(pltpu.with_memory_space_constraint(a, pltpu.HBM) for a in args)
    vmem = pl.BlockSpec(memory_space=pltpu.VMEM)
    specs = [pl.BlockSpec(memory_space=pltpu.HBM) if off_chip else vmem] * len(args)
    if scalar:
        specs[0] = pl.BlockSpec(memory_space=pltpu.SMEM)
    size = sum(a.size * a.dtype.itemsize for a in (*args, *outs))
    return pl.pallas_call(
        kernel,
        out_shape=outs,
        in_specs=specs,
        out_specs=tuple([vmem] * len(outs)),
        scratch_shapes=list(scratch),
        cost_estimate=pl.CostEstimate(flops=flops, bytes_accessed=size, transcendentals=0),
        compiler_params=pltpu.CompilerParams(vmem_limit_bytes=32 << 20),
    )(*args)


def swap(value, axis, bit):
    return lax.ppermute(value, axis, [(i, i ^ bit) for i in range(lax.axis_size(axis))])


def gathered(value, axis):
    bit = 1
    while bit < lax.axis_size(axis):
        value = jnp.concatenate([value, swap(value, axis, bit)], axis=1)
        bit *= 2
    return value


def owned_sum(value, axis):
    bit = lax.axis_size(axis) // 2
    while bit:
        mine, theirs = jnp.split(value, 2, axis=1)
        value = mine + swap(theirs, axis, bit)
        bit //= 2
    return value


def total_sum(value, axis):
    bit = 1
    while bit < lax.axis_size(axis):
        value = value + swap(value, axis, bit)
        bit *= 2
    return value


def planned(mesh_size):
    return mesh_size == 8


def chip_carries(total, size):
    n = lax.axis_size("ctx")
    place = lax.axis_index("ctx")

    def state(v):
        return v[..., :size, :]

    def decay(v):
        return v[..., size : size + 1, :]

    fwd, bwd = total[0], total[1]
    ahead = behind = jnp.zeros_like(state(fwd))
    ahead_decay = behind_decay = jnp.ones_like(decay(fwd))
    bit = 2
    while bit < n:
        o_fwd, o_bwd = swap(fwd, "ctx", bit), swap(bwd, "ctx", bit)
        up = (place & bit) != 0
        ahead = jnp.where(up, ahead + ahead_decay * state(o_fwd), ahead)
        ahead_decay = jnp.where(up, ahead_decay * decay(o_fwd), ahead_decay)
        behind = jnp.where(up, behind, behind + behind_decay * state(o_bwd))
        behind_decay = jnp.where(up, behind_decay, behind_decay * decay(o_bwd))
        both = fwd[..., size:, :] * o_fwd[..., size:, :]
        f1, f2 = jnp.where(up, o_fwd, fwd), jnp.where(up, fwd, o_fwd)
        b1, b2 = jnp.where(up, o_bwd, bwd), jnp.where(up, bwd, o_bwd)
        fwd = jnp.concatenate([state(f2) + decay(f2) * state(f1), both], axis=-2)
        bwd = jnp.concatenate([state(b1) + decay(b1) * state(b2), both], axis=-2)
        bit *= 2
    return ahead, behind


def local(x, b, r, raw, rate, bias, skip, g):
    return layer(x[0], b[0], r[0], raw[0], rate, bias, skip, g[0])


def spread_generally(own, mate, size):
    odd = (lax.axis_index("ctx") & 1) == 1
    s_o, g_o, a_o = own[0, :, :size], own[1, :, :size], own[0, :, size:]
    s_p, g_p, a_p = mate[0, :, :size], mate[1, :, :size], mate[0, :, size:]
    fwd = jnp.where(odd, a_o[:, :1] * s_p + s_o, a_p[:, :1] * s_o + s_p)
    bwd = jnp.where(odd, g_p + a_p[:, :1] * g_o, g_o + a_o[:, :1] * g_p)
    decay = a_o * a_p
    chip = jnp.stack([jnp.concatenate([fwd, decay], axis=1), jnp.concatenate([bwd, decay], axis=1)])
    ahead, behind = chip_carries(chip, size)
    through = jnp.where(odd, a_p[:, :1], a_o[:, :1]) * ahead + jnp.where(odd, s_p, s_o)
    theirs = jnp.stack([jnp.where(odd, ahead, through), jnp.where(odd, g_o + a_o[:, :1] * behind, behind)])
    mine = jnp.stack([jnp.where(odd, through, ahead), jnp.where(odd, behind, g_p + a_p[:, :1] * behind)])
    return mine, theirs


def spread_planned(place, own, mate, size):
    part = own.shape[-1]
    message = jax.ShapeDtypeStruct((size + PAD, part), F32)
    row = jax.ShapeDtypeStruct((size, part), F32)
    ends = jax.ShapeDtypeStruct((PAD, part), F32)
    both = jax.ShapeDtypeStruct((2, 2, size, part), F32)
    to_xa, to_yb, to_late, to_diag, kept = call(
        totals_kernel, (message, message, message, ends, message), (place, own, mate), scalar=True
    )
    diag = swap(to_diag, "ctx", 6)
    xa = swap(to_xa, "ctx", 2)
    yb = swap(to_yb, "ctx", 4)
    late = swap(to_late, "ctx", 2)
    (to_ya,) = call(row_kernel, (row,), (place, to_xa, xa), scalar=True)
    ya = swap(to_ya, "ctx", 4)
    (to_xb,) = call(onward_kernel, (message,), (place, kept, diag, yb), scalar=True)
    xb = swap(to_xb, "ctx", 2)
    return call(reach_kernel, (both, both), (place, own, mate, xa, yb, late, ya, xb), scalar=True)


def layer(x, b, r, raw, rate, bias, skip, g):
    heads, count = raw.shape
    total, size = x.shape[1], b.shape[1]
    half = total // 2
    part = half // 2
    groups = lax.axis_size("dp")
    shape = jax.ShapeDtypeStruct
    place = jnp.stack([lax.axis_index("ctx"), lax.axis_index("dp")]).astype(jnp.int32)
    got = gathered(jnp.stack([rate, bias, skip]), "dp")
    message = shape((2, 2, size + PAD, part), F32)
    small = shape((heads, count), F32)
    wide = shape((count, total), F32)
    square = shape((count, size), F32)
    mixed = shape((count, count), F32)
    columns = shape((heads, LANES), F32)
    args = (x, g, b, r, raw)
    x, g, b, r, raw = call(
        prep_kernel, tuple(shape(v.shape, v.dtype) for v in args), args,
        scratch=[pltpu.SemaphoreType.DMA((len(args),))], off_chip=True,
    )
    own, oth, cum, step, par = call(
        functools.partial(ends_kernel, groups),
        (message, message, small, small, columns), (place, x, g, b, r, raw, got),
        scratch=[pltpu.VMEM((heads, LANES), F32)], flops=10**9, scalar=True,
    )
    mate = swap(oth, "ctx", 1)
    if planned(lax.axis_size("ctx")):
        mine, theirs = spread_planned(place, own, mate, size)
    else:
        mine, theirs = spread_generally(own, mate, size)
    gram, gram_t = call(gram_kernel, (mixed, mixed), (b, r), flops=10**7)
    inner, dxin, db0, dc0 = call(
        inside_kernel,
        (wide, wide, square, square),
        (x, g, b, r, cum, step, gram, gram_t),
        scratch=[pltpu.VMEM((count, LANES), F32), pltpu.VMEM((count, count), F32)],
        flops=10**9,
    )
    rest = swap(theirs, "ctx", 1)
    ready = (place, x, g, b, r, raw, par, inner, dxin)
    halved = shape((count, half), BF16)
    whole = shape((count, total), BF16)
    y0, dx0, uv, sums, db1, dc1 = call(
        first_kernel,
        (halved, halved, shape((2 * count, heads), F32), shape((3 * PAD, heads), F32), square, square),
        (*ready, mine, cum, step, db0, dc0), flops=10**9, scalar=True,
    )
    y1, dx1, draw, tot = call(
        functools.partial(second_kernel, groups), (halved, halved, small, shape((PAD, heads), F32)),
        (*ready, rest, uv, sums),
        scratch=[pltpu.VMEM((heads, LANES), F32), pltpu.VMEM((heads, LANES), F32)], flops=10**9, scalar=True,
    )
    owned = owned_sum(total_sum(tot, "ctx"), "dp")
    y, dx, db, dc = call(
        third_kernel, (whole, whole, square, square),
        (place, x, g, cum, step, rest, db1, dc1, y0, dx0, y1, dx1), flops=10**9, scalar=True,
    )
    return (y[None], dx[None], db[None], dc[None], draw[None], owned[0], owned[1], owned[2])


def solution(mesh):
    wide = P("dp", "ctx", None)
    strides = P("dp", None, "ctx")
    return jax.shard_map(
        local,
        mesh=mesh,
        in_specs=(wide, wide, wide, strides, P("dp"), P("dp"), P("dp"), wide),
        out_specs=(wide, wide, wide, wide, strides, P("dp"), P("dp"), P("dp")),
        check_vma=False,
    )
```

```python
import functools

import jax
import jax.numpy as jnp
from jax import lax
from jax.experimental import pallas as pl
from jax.experimental.pallas import tpu as pltpu
from jax.sharding import PartitionSpec as P


F32, BF16 = jnp.float32, jnp.bfloat16
EXACT = lax.Precision.HIGHEST
NT = (((1,), (1,)), ((), ()))
NN = (((1,), (0,)), ((), ()))
LANES = 128
PAD = 8


def mm(a, b, dims=NN):
    return lax.dot_general(a, b, dims, preferred_element_type=F32)


def exact_mm(a, b, dims=NN):
    return lax.dot_general(a, b, dims, precision=EXACT, preferred_element_type=F32)


def split(v):
    hi = v.astype(BF16)
    return hi, (v - hi.astype(F32)).astype(BF16)


def spread(heads, width, first, lanes):
    head = lax.broadcasted_iota(jnp.int32, (heads, lanes), 0)
    lane = lax.broadcasted_iota(jnp.int32, (heads, lanes), 1) + first
    inside = jnp.logical_and(lane >= head * width, lane < head * width + width)
    return jnp.where(inside, 1.0, 0.0).astype(BF16)


def expand(per_head, hot):
    hi, lo = split(per_head)
    return mm(jnp.concatenate([hi, lo], axis=1), jnp.concatenate([hot, hot], axis=0))


def relative(n, place, block, src_ref, dst_ref):
    for i in range(n):
        dst_ref[pl.ds(i * block, block), :] = src_ref[pl.ds(pl.multiple_of((place ^ i) * block, block), block), :]


def scans(raw, par):
    rate, bias = par[:, 0:1], par[:, 1:2]
    z = raw + bias
    step = jnp.maximum(z, 0.0) + jnp.log1p(jnp.exp(-jnp.abs(z)))
    scale = -jnp.exp(rate)
    logdecay = scale * step
    count = raw.shape[1]
    early = lax.broadcasted_iota(jnp.int32, (count, count), 0)
    late = lax.broadcasted_iota(jnp.int32, (count, count), 1)
    upper = jnp.where(early <= late, 1.0, 0.0)
    cum = exact_mm(logdecay, upper)
    return z, step, scale, logdecay, cum, upper


def prep_kernel(x_ref, g_ref, b_ref, r_ref, raw_ref, *rest):
    outs, sems = rest[:5], rest[5]
    copies = [
        pltpu.make_async_copy(src, dst, sems.at[k])
        for k, (src, dst) in enumerate(zip((x_ref, g_ref, b_ref, r_ref, raw_ref), outs))
    ]
    for copy in copies:
        copy.start()
    for copy in copies:
        copy.wait()


def ends_kernel(
    groups, x_ref, g_ref, b_ref, r_ref, raw_ref, got_ref, own_ref, oth_ref, cum_ref, step_ref, par_ref, mixed_ref,
):
    heads, count = raw_ref.shape
    rows = got_ref.shape[0]
    mixed_ref[...] = jnp.concatenate([got_ref[...], jnp.zeros((LANES - rows, heads), F32)], axis=0).T
    relative(groups, lax.axis_index("dp"), heads // groups, mixed_ref, par_ref)
    total = x_ref.shape[1]
    half = total // 2
    width = total // heads
    part = half // 2
    _, step, _, _, cum, _ = scans(raw_ref[...], par_ref[...])
    cum_ref[...] = cum
    step_ref[...] = step
    tail = (jnp.exp(cum[:, -1:] - cum) * step).T
    grow = jnp.exp(cum).T
    bt = b_ref[...].astype(F32).T.astype(BF16)
    ct = r_ref[...].astype(F32).T.astype(BF16)
    bt2 = jnp.concatenate([bt, bt], axis=1)
    ct2 = jnp.concatenate([ct, ct], axis=1)
    c = lax.axis_index("ctx") & 1
    size = b_ref.shape[1]
    for which, out in ((1 - c, oth_ref), (c, own_ref)):
        for k in range(2):
            first = pl.multiple_of(which * half + k * part, part)
            hot = spread(heads, width, first, part)
            here = pl.ds(first, part)
            grow_x = expand(grow, hot)
            xt = expand(tail, hot) * x_ref[:, here].astype(F32)
            out[0, k, :size] = mm(bt2, jnp.concatenate(split(xt), axis=0))
            gt = grow_x * g_ref[:, here].astype(F32)
            out[1, k, :size] = mm(ct2, jnp.concatenate(split(gt), axis=0))
            last = jnp.broadcast_to(grow_x[count - 1 :, :], (PAD, part))
            out[0, k, size:] = last
            out[1, k, size:] = last


def totals_kernel(own_ref, mate_ref, xa_ref, yb_ref, late_ref, diag_ref, kept_ref):
    place = lax.axis_index("ctx")
    odd, x1, y1 = (place & 1) != 0, (place >> 1) & 1, (place >> 2) & 1
    size = own_ref.shape[2] - PAD

    def total(way, part, first, second, out):
        f, l = first[way, part, :size], second[way, part, :size]
        fd, ld = first[way, part, size:], second[way, part, size:]
        lead = jnp.broadcast_to((way == 0).astype(F32), fd[:1].shape)
        keep = jnp.where(lead > 0.0, ld[:1], 1.0)
        onto = jnp.where(lead > 0.0, 1.0, fd[:1])
        out[:size] = keep * f + onto * l
        out[size:] = fd * ld

    def all_totals(first, second):
        total(y1, 0, first, second, xa_ref)
        total(y1, 1, first, second, yb_ref)
        total(1 - y1, 1, first, second, kept_ref)

        @pl.when(x1 != y1)
        def _():
            total(1 - y1, 0, first, second, late_ref)

        @pl.when(x1 == y1)
        def _():
            late_ref[...] = yb_ref[...]

        diag_ref[...] = kept_ref[size:]

    @pl.when(odd)
    def _():
        all_totals(mate_ref, own_ref)

    @pl.when(jnp.logical_not(odd))
    def _():
        all_totals(own_ref, mate_ref)


def row_kernel(sent_ref, xa_ref, row_ref):
    place = lax.axis_index("ctx")
    x1, y1 = (place >> 1) & 1, (place >> 2) & 1
    size = row_ref.shape[0]

    @pl.when(x1 != y1)
    def _():
        row_ref[...] = sent_ref[:size] + sent_ref[size : size + 1] * xa_ref[:size]

    @pl.when(x1 == y1)
    def _():
        row_ref[...] = xa_ref[:size] + xa_ref[size : size + 1] * sent_ref[:size]


def onward_kernel(kept_ref, diag_ref, yb_ref, xb_ref):
    place = lax.axis_index("ctx")
    x1, y1 = (place >> 1) & 1, (place >> 2) & 1
    size = xb_ref.shape[0] - PAD

    @pl.when(x1 != y1)
    def _():
        xb_ref[:size] = kept_ref[:size] + kept_ref[size : size + 1] * diag_ref[:1] * yb_ref[:size]
        xb_ref[size:] = kept_ref[size:]

    @pl.when(x1 == y1)
    def _():
        xb_ref[...] = yb_ref[...]


def reach_kernel(own_ref, mate_ref, xa_ref, yb_ref, late_ref, ya_ref, xb_ref, mine_ref, rest_ref):
    place = lax.axis_index("ctx")
    odd, x1, y1 = (place & 1) != 0, (place >> 1) & 1, (place >> 2) & 1
    size = ya_ref.shape[0]

    def spread_to(first, second, to_first, to_second):
        for part in range(2):
            if part == 0:
                bent_far, near = ya_ref[...], xa_ref
                flat_far = late_ref[:size] + late_ref[size : size + 1] * ya_ref[...]
                far = jnp.where(jnp.broadcast_to(x1 != y1, flat_far.shape), bent_far, flat_far)
            else:
                near = late_ref
                far = xb_ref[:size] + xb_ref[size : size + 1] * yb_ref[:size]
            near = jnp.where(jnp.broadcast_to(x1 != y1, far.shape), near[:size], 0.0)
            forward = jnp.broadcast_to(y1 == 1, far.shape)
            ahead, behind = jnp.where(forward, far, near), jnp.where(forward, near, far)
            to_first[0, part] = ahead
            to_second[0, part] = first[0, part, size : size + 1] * ahead + first[0, part, :size]
            to_second[1, part] = behind
            to_first[1, part] = second[1, part, size : size + 1] * behind + second[1, part, :size]

    @pl.when(odd)
    def _():
        spread_to(mate_ref, own_ref, rest_ref, mine_ref)

    @pl.when(jnp.logical_not(odd))
    def _():
        spread_to(own_ref, mate_ref, mine_ref, rest_ref)


def inside_kernel(own, last, x_ref, g_ref, b_ref, r_ref, cum_ref, step_ref, *refs):
    heads, count = cum_ref.shape
    if last:
        dgram0_ref, inner_ref, dxin_ref, db_ref, dc_ref, cumt_ref, dgram_ref = refs
    else:
        inner_ref, dxin_ref, dgram_ref, cumt_ref = refs
    half = inner_ref.shape[1]
    width = 2 * half // heads
    pack = LANES // width
    core = lax.axis_index("ctx") & 1
    base = (core if own else 1 - core) * (half // LANES)
    t_row = lax.broadcasted_iota(jnp.int32, (count, count), 0)
    t_col = lax.broadcasted_iota(jnp.int32, (count, count), 1)
    b, r = b_ref[...], r_ref[...]
    gram = jnp.where(t_row >= t_col, mm(r, b, NT), 0.0)
    gram_t = jnp.where(t_row <= t_col, mm(b, r, NT), 0.0)
    cumt_ref[...] = jnp.concatenate([cum_ref[...], jnp.zeros((LANES - heads, count), F32)], axis=0).T
    step_t = step_ref[...].T
    dgram_ref[...] = dgram0_ref[...] if last else jnp.zeros_like(dgram_ref)
    lane = lax.broadcasted_iota(jnp.int32, (count, LANES), 1)

    def group(k, _):
        j = base + k
        at = pl.multiple_of(j * LANES, LANES)
        out = pl.ds(pl.multiple_of(k * LANES, LANES), LANES)
        x4 = x_ref[:, pl.ds(at, LANES)]
        g4 = g_ref[:, pl.ds(at, LANES)]
        cols = pltpu.roll(cumt_ref[...], LANES - j * pack, 1)
        his, los, thi, tlo, xs, gs = [], [], [], [], [], []
        dgram = dgram_ref[...]
        for i in range(pack):
            head = j * pack + i
            row = cum_ref[pl.ds(head, 1), :]
            step_row = step_ref[pl.ds(head, 1), :]
            diff = cols[:, i : i + 1] - row
            seg = jnp.exp(jnp.minimum(diff, 0.0)) * step_row
            seg_t = jnp.exp(jnp.minimum(-diff, 0.0))
            mine = jnp.logical_and(lane >= i * width, lane < (i + 1) * width)
            xm = jnp.where(mine, x4.astype(F32), 0.0).astype(BF16)
            gm = jnp.where(mine, g4.astype(F32), 0.0).astype(BF16)
            dgram = dgram + mm(gm, x4, NT) * seg
            hi, lo = split(gram * seg)
            his.append(hi)
            los.append(lo)
            hi, lo = split(gram_t * seg_t)
            thi.append(hi)
            tlo.append(lo)
            xs.append(xm)
            gs.append(gm)
        dgram_ref[...] = dgram
        inner_ref[:, out] = mm(jnp.concatenate(his + los, axis=1), jnp.concatenate(xs + xs, axis=0))
        hot = spread(heads, width, at, LANES)
        back = mm(jnp.concatenate(thi + tlo, axis=1), jnp.concatenate(gs + gs, axis=0))
        dxin_ref[:, out] = back * expand(step_t, hot)
        return 0

    lax.fori_loop(0, half // LANES, group, 0)
    if last:
        dgram = jnp.where(t_row >= t_col, dgram_ref[...], 0.0)
        hi, lo = split(dgram)
        dc_ref[...] = mm(jnp.concatenate([hi, lo], axis=1), jnp.concatenate([b, b], axis=0))
        hi, lo = split(dgram.T)
        db_ref[...] = mm(jnp.concatenate([hi, lo], axis=1), jnp.concatenate([r, r], axis=0))


def lanes_of(heads, total, which):
    half = total // 2
    part = half // 2
    for k in range(2):
        first = pl.multiple_of(which * half + k * part, part)
        yield k, pl.ds(first, part), pl.ds(k * part, part), spread(heads, total // heads, first, part)


def carried(which, src, x_ref, g_ref, b_ref, r_ref, raw, par, inner_ref, dxin_ref, uv, sums, y_ref, dx_ref):
    heads, _ = raw.shape
    scanned = scans(raw, par)
    _, step, _, _, cum, _ = scanned
    tail = (jnp.exp(cum[:, -1:] - cum) * step).T
    grow = jnp.exp(cum).T
    skip = jnp.broadcast_to(par[:, 2:3], (heads, LANES)).T[:PAD]
    b, r = b_ref[...], r_ref[...]
    b2 = jnp.concatenate([b, b], axis=1)
    r2 = jnp.concatenate([r, r], axis=1)
    for k, here, out, hot in lanes_of(heads, x_ref.shape[1], which):
        x = x_ref[:, here].astype(F32)
        g = g_ref[:, here].astype(F32)
        grow_x, tail_x, skip_x = expand(grow, hot), expand(tail, hot), expand(skip, hot)[0:1]
        before, later = src[0, k], src[1, k]
        flow = inner_ref[:, out] + grow_x * mm(r2, jnp.concatenate(split(before), axis=0))
        y_ref[:, out] = (flow + skip_x * x).astype(BF16)
        reach = tail_x * mm(b2, jnp.concatenate(split(later), axis=0))
        back = dxin_ref[:, out] + reach
        dx_ref[:, out] = (back + skip_x * g).astype(BF16)
        uv_hi, uv_lo = split(jnp.concatenate([g * flow, x * back], axis=0))
        uv = uv + mm(uv_hi, hot, NT) + mm(uv_lo, hot, NT)
        parts = jnp.concatenate(
            [jnp.sum(v.reshape(-1, PAD, v.shape[1]), axis=0) for v in (x * reach, before * later, g * x)], axis=0
        )
        s_hi, s_lo = split(parts)
        sums = sums + mm(s_hi, hot, NT) + mm(s_lo, hot, NT)
    return uv, sums, scanned


def projected(which, src, x_ref, g_ref, cum, step, db, dc):
    tail = (jnp.exp(cum[:, -1:] - cum) * step).T
    grow = jnp.exp(cum).T
    for k, here, _, hot in lanes_of(cum.shape[0], x_ref.shape[1], which):
        h_hi, h_lo = split(src[0, k])
        d_hi, d_lo = split(src[1, k])
        e_hi, e_lo = split(expand(grow, hot) * g_ref[:, here].astype(F32))
        dc = dc + mm(e_hi, h_hi, NT) + mm(e_hi, h_lo, NT) + mm(e_lo, h_hi, NT)
        t_hi, t_lo = split(expand(tail, hot) * x_ref[:, here].astype(F32))
        db = db + mm(t_hi, d_hi, NT) + mm(t_hi, d_lo, NT) + mm(t_lo, d_hi, NT)
    return db, dc


def first_kernel(
    x_ref, g_ref, b_ref, r_ref, raw_ref, par_ref, inner_ref, dxin_ref, src_ref, cum_ref, step_ref,
    db0_ref, dc0_ref, y_ref, dx_ref, uv_ref, sums_ref, db_ref, dc_ref,
):
    c = lax.axis_index("ctx") & 1
    uv, sums = jnp.zeros(uv_ref.shape, F32), jnp.zeros(sums_ref.shape, F32)
    uv_ref[...], sums_ref[...], _ = carried(
        c, src_ref, x_ref, g_ref, b_ref, r_ref, raw_ref[...], par_ref[...], inner_ref, dxin_ref, uv, sums, y_ref, dx_ref
    )
    db_ref[...], dc_ref[...] = projected(
        c, src_ref, x_ref, g_ref, cum_ref[...], step_ref[...], db0_ref[...], dc0_ref[...]
    )


def second_kernel(
    groups, x_ref, g_ref, b_ref, r_ref, raw_ref, par_ref, inner_ref, dxin_ref, src_ref,
    uv0_ref, sums0_ref, y_ref, dx_ref, draw_ref, tot_ref, col_ref, rel_ref,
):
    heads, count = raw_ref.shape
    other = 1 - (lax.axis_index("ctx") & 1)
    uv, sums, (z, step, scale, logdecay, cum, upper) = carried(
        other, src_ref, x_ref, g_ref, b_ref, r_ref, raw_ref[...], par_ref[...], inner_ref, dxin_ref,
        uv0_ref[...], sums0_ref[...], y_ref, dx_ref,
    )
    u = uv[:count].T
    v = uv[count:].T
    sums_t = sums.T
    reach_sum = jnp.sum(sums_t[:, :PAD], axis=1, keepdims=True)
    meet_sum = jnp.sum(sums_t[:, PAD : 2 * PAD], axis=1, keepdims=True)
    skip_sum = jnp.sum(sums_t[:, 2 * PAD :], axis=1, keepdims=True)
    end = reach_sum + jnp.exp(cum[:, -1:]) * meet_sum
    dlog = exact_mm(u - v, upper, NT) + end
    draw = (scale * dlog + v / step) * jax.nn.sigmoid(z)
    draw_ref[...] = draw
    column = lax.broadcasted_iota(jnp.int32, (heads, LANES), 1)
    rate_sum = jnp.sum(dlog * logdecay, axis=1, keepdims=True)
    bias_sum = jnp.sum(draw, axis=1, keepdims=True)
    col_ref[...] = jnp.where(column == 0, rate_sum, jnp.where(column == 1, bias_sum, jnp.where(column == 2, skip_sum, 0.0)))
    relative(groups, lax.axis_index("dp"), heads // groups, col_ref, rel_ref)
    tot_ref[...] = rel_ref[...].T[:PAD]


def third_kernel(
    x_ref, g_ref, cum_ref, step_ref, src_ref, db0_ref, dc0_ref, y0_ref, dx0_ref, y1_ref, dx1_ref,
    y_ref, dx_ref, db_ref, dc_ref,
):
    c = lax.axis_index("ctx") & 1
    half = x_ref.shape[1] // 2
    for which, ys, dxs in ((c, y0_ref, dx0_ref), (1 - c, y1_ref, dx1_ref)):
        at = pl.ds(pl.multiple_of(which * half, half), half)
        y_ref[:, at] = ys[...]
        dx_ref[:, at] = dxs[...]
    db_ref[...], dc_ref[...] = projected(
        1 - c, src_ref, x_ref, g_ref, cum_ref[...], step_ref[...], db0_ref[...], dc0_ref[...]
    )


def call(kernel, outs, args, scratch=(), flops=0, off_chip=False):
    if off_chip:
        args = tuple(pltpu.with_memory_space_constraint(a, pltpu.HBM) for a in args)
    vmem = pl.BlockSpec(memory_space=pltpu.VMEM)
    specs = [pl.BlockSpec(memory_space=pltpu.HBM) if off_chip else vmem] * len(args)
    size = sum(a.size * a.dtype.itemsize for a in (*args, *outs))
    return pl.pallas_call(
        kernel,
        out_shape=outs,
        in_specs=specs,
        out_specs=tuple([vmem] * len(outs)),
        scratch_shapes=list(scratch),
        cost_estimate=pl.CostEstimate(flops=flops, bytes_accessed=size, transcendentals=0),
        compiler_params=pltpu.CompilerParams(vmem_limit_bytes=32 << 20),
    )(*args)


def swap(value, axis, bit):
    return lax.ppermute(value, axis, [(i, i ^ bit) for i in range(lax.axis_size(axis))])


def gathered(value, axis):
    bit = 1
    while bit < lax.axis_size(axis):
        value = jnp.concatenate([value, swap(value, axis, bit)], axis=1)
        bit *= 2
    return value


def owned_sum(value, axis):
    bit = lax.axis_size(axis) // 2
    while bit:
        mine, theirs = jnp.split(value, 2, axis=1)
        value = mine + swap(theirs, axis, bit)
        bit //= 2
    return value


def total_sum(value, axis):
    bit = 1
    while bit < lax.axis_size(axis):
        value = value + swap(value, axis, bit)
        bit *= 2
    return value


def planned(mesh_size):
    return mesh_size == 8


def chip_carries(total, size):
    n = lax.axis_size("ctx")
    place = lax.axis_index("ctx")

    def state(v):
        return v[..., :size, :]

    def decay(v):
        return v[..., size : size + 1, :]

    fwd, bwd = total[0], total[1]
    ahead = behind = jnp.zeros_like(state(fwd))
    ahead_decay = behind_decay = jnp.ones_like(decay(fwd))
    bit = 2
    while bit < n:
        o_fwd, o_bwd = swap(fwd, "ctx", bit), swap(bwd, "ctx", bit)
        up = (place & bit) != 0
        ahead = jnp.where(up, ahead + ahead_decay * state(o_fwd), ahead)
        ahead_decay = jnp.where(up, ahead_decay * decay(o_fwd), ahead_decay)
        behind = jnp.where(up, behind, behind + behind_decay * state(o_bwd))
        behind_decay = jnp.where(up, behind_decay, behind_decay * decay(o_bwd))
        both = fwd[..., size:, :] * o_fwd[..., size:, :]
        f1, f2 = jnp.where(up, o_fwd, fwd), jnp.where(up, fwd, o_fwd)
        b1, b2 = jnp.where(up, o_bwd, bwd), jnp.where(up, bwd, o_bwd)
        fwd = jnp.concatenate([state(f2) + decay(f2) * state(f1), both], axis=-2)
        bwd = jnp.concatenate([state(b1) + decay(b1) * state(b2), both], axis=-2)
        bit *= 2
    return ahead, behind


def local(x, b, r, raw, rate, bias, skip, g):
    return layer(x[0], b[0], r[0], raw[0], rate, bias, skip, g[0])


def spread_generally(own, mate, size):
    odd = (lax.axis_index("ctx") & 1) == 1
    s_o, g_o, a_o = own[0, :, :size], own[1, :, :size], own[0, :, size:]
    s_p, g_p, a_p = mate[0, :, :size], mate[1, :, :size], mate[0, :, size:]
    fwd = jnp.where(odd, a_o[:, :1] * s_p + s_o, a_p[:, :1] * s_o + s_p)
    bwd = jnp.where(odd, g_p + a_p[:, :1] * g_o, g_o + a_o[:, :1] * g_p)
    decay = a_o * a_p
    chip = jnp.stack([jnp.concatenate([fwd, decay], axis=1), jnp.concatenate([bwd, decay], axis=1)])
    ahead, behind = chip_carries(chip, size)
    through = jnp.where(odd, a_p[:, :1], a_o[:, :1]) * ahead + jnp.where(odd, s_p, s_o)
    theirs = jnp.stack([jnp.where(odd, ahead, through), jnp.where(odd, g_o + a_o[:, :1] * behind, behind)])
    mine = jnp.stack([jnp.where(odd, through, ahead), jnp.where(odd, behind, g_p + a_p[:, :1] * behind)])
    return mine, theirs


def spread_planned(own, mate, size):
    part = own.shape[-1]
    message = jax.ShapeDtypeStruct((size + PAD, part), F32)
    row = jax.ShapeDtypeStruct((size, part), F32)
    ends = jax.ShapeDtypeStruct((PAD, part), F32)
    both = jax.ShapeDtypeStruct((2, 2, size, part), F32)
    to_xa, to_yb, to_late, to_diag, kept = call(totals_kernel, (message, message, message, ends, message), (own, mate))
    diag = swap(to_diag, "ctx", 6)
    xa = swap(to_xa, "ctx", 2)
    yb = swap(to_yb, "ctx", 4)
    late = swap(to_late, "ctx", 2)
    (to_ya,) = call(row_kernel, (row,), (to_xa, xa))
    ya = swap(to_ya, "ctx", 4)
    (to_xb,) = call(onward_kernel, (message,), (kept, diag, yb))
    xb = swap(to_xb, "ctx", 2)
    return call(reach_kernel, (both, both), (own, mate, xa, yb, late, ya, xb))


def layer(x, b, r, raw, rate, bias, skip, g):
    heads, count = raw.shape
    total, size = x.shape[1], b.shape[1]
    half = total // 2
    part = half // 2
    groups = lax.axis_size("dp")
    shape = jax.ShapeDtypeStruct
    got = gathered(jnp.stack([rate, bias, skip]), "dp")
    message = shape((2, 2, size + PAD, part), F32)
    small = shape((heads, count), F32)
    square = shape((count, size), F32)
    mixed = shape((count, count), F32)
    columns = shape((heads, LANES), F32)
    args = (x, g, b, r, raw)
    x, g, b, r, raw = call(
        prep_kernel, tuple(shape(v.shape, v.dtype) for v in args), args,
        scratch=[pltpu.SemaphoreType.DMA((len(args),))], off_chip=True,
    )
    own, oth, cum, step, par = call(
        functools.partial(ends_kernel, groups),
        (message, message, small, small, columns), (x, g, b, r, raw, got),
        scratch=[pltpu.VMEM((heads, LANES), F32)], flops=10**9,
    )
    mate = swap(oth, "ctx", 1)
    if planned(lax.axis_size("ctx")):
        mine, theirs = spread_planned(own, mate, size)
    else:
        mine, theirs = spread_generally(own, mate, size)
    halves = shape((count, half), F32)
    inner0, dxin0, dgram = call(
        functools.partial(inside_kernel, True, False), (halves, halves, mixed), (x, g, b, r, cum, step),
        scratch=[pltpu.VMEM((count, LANES), F32)], flops=10**9,
    )
    inner1, dxin1, db0, dc0 = call(
        functools.partial(inside_kernel, False, True), (halves, halves, square, square),
        (x, g, b, r, cum, step, dgram),
        scratch=[pltpu.VMEM((count, LANES), F32), pltpu.VMEM((count, count), F32)], flops=10**9,
    )
    rest = swap(theirs, "ctx", 1)
    ready = (x, g, b, r, raw, par)
    halved = shape((count, half), BF16)
    whole = shape((count, total), BF16)
    y0, dx0, uv, sums, db1, dc1 = call(
        first_kernel,
        (halved, halved, shape((2 * count, heads), F32), shape((3 * PAD, heads), F32), square, square),
        (*ready, inner0, dxin0, mine, cum, step, db0, dc0), flops=10**9,
    )
    y1, dx1, draw, tot = call(
        functools.partial(second_kernel, groups), (halved, halved, small, shape((PAD, heads), F32)),
        (*ready, inner1, dxin1, rest, uv, sums),
        scratch=[pltpu.VMEM((heads, LANES), F32), pltpu.VMEM((heads, LANES), F32)], flops=10**9,
    )
    owned = owned_sum(total_sum(tot, "ctx"), "dp")
    y, dx, db, dc = call(
        third_kernel, (whole, whole, square, square),
        (x, g, cum, step, rest, db1, dc1, y0, dx0, y1, dx1), flops=10**9,
    )
    return (y[None], dx[None], db[None], dc[None], draw[None], owned[0], owned[1], owned[2])


def solution(mesh):
    wide = P("dp", "ctx", None)
    strides = P("dp", None, "ctx")
    return jax.shard_map(
        local,
        mesh=mesh,
        in_specs=(wide, wide, wide, strides, P("dp"), P("dp"), P("dp"), wide),
        out_specs=(wide, wide, wide, wide, strides, P("dp"), P("dp"), P("dp")),
        check_vma=False,
    )
```
